32 devices in a mesh: tm: 8 (over z, y), pair: 4 (over x, core).
Axes of the slice: x: 2, y: 2, z: 4, core: 2. Of those that a mesh axis runs over, the one named last changes fastest.
Arguments:
- x_series: float32 [128, 32768], P('pair', 'tm'), may hold values from -6 to 6
- y_series: float32 [128, 32768], P('pair', 'tm'), may hold values from -6 to 6
Outputs:
- correlation: float32 [128, 512], P('tm', 'pair')
The draws below stay inside these ranges and needn't reach their ends.
All inputs are finite; a program needn't handle non-finite values.
Results may differ from the reference program's by a relative error of at most 0.000082.
Values sent between devices are 32-bit elements; how exact they have to be, the bound alone decides.
No kernel may reach another device: no remote copies, remote signals or barrier semaphores. Data moves between devices by JAX's collectives and lax.ppermute only.
A program may use at most 64 MiB of HBM per device.

```python
import math
import jax
import jax.numpy as jnp
from jax import lax

L = 512
PAIRS = 128
NT = 32768


def block_scale(own_key, extent, cuts, low, largest):
    level = 1.0
    for axis_at, parts in cuts:
        steps = jax.random.uniform(jax.random.fold_in(jax.random.fold_in(own_key, 6), axis_at), (parts,), jnp.float32, low / len(cuts), largest / len(cuts))
        level = level * jnp.repeat(jnp.exp(steps), extent[axis_at] // parts).reshape((-1,) + (1,) * (len(extent) - 1 - axis_at))
    return level


def bell_draw(stream_key, dims, width, most, cuts=(), held_as=jnp.bfloat16):
    result = jax.random.normal(stream_key, dims, jnp.float32) * width
    if len(cuts) > 0:
        result = block_scale(stream_key, dims, cuts, -0.22, 0.18) * result
    return jnp.clip(result, min=-most, max=most).astype(held_as)


def setup_inputs(seed: int = 0) -> dict:
    splits = jax.random.split(jax.random.key(seed), 3)
    return {
        "x_series": bell_draw(splits[0], (PAIRS, NT), 1.0, 6.0, ((0, 4), (1, 8)), jnp.float32),
        "y_series": bell_draw(splits[1], (PAIRS, NT), 1.0, 6.0, ((0, 4), (1, 8)), jnp.float32),
    }


def lag_products(series, extended):
    block_len = min(128, L)
    pair_count, length = series.shape
    block_rows = length // block_len
    left_rows = series.reshape(pair_count, block_rows, block_len)
    pieces = [extended[:, offset * block_len:offset * block_len + length].reshape(pair_count, block_rows, block_len) for offset in range(L // block_len + 1)]
    right_rows = jnp.concatenate(pieces, axis=2)
    grams = jnp.einsum('pbi,pbj->pij', left_rows, right_rows, precision=lax.Precision.HIGHEST, preferred_element_type=jnp.float32)
    span_cols = L + block_len
    flattened = grams.reshape(pair_count, block_len * span_cols)
    flattened = jnp.pad(flattened, ((0, 0), (0, block_len)))
    skewed = flattened.reshape(pair_count, block_len, span_cols + 1)
    return lax.optimization_barrier(jnp.sum(skewed[:, :, :L], axis=1))

def per_block(members):
    return lag_products(members[0], members[1])

def reference(x_series, y_series):
    extended = jnp.pad(y_series, ((0, 0), (0, L)))
    block_count = PAIRS // 8
    totals = lax.map(per_block, (x_series.reshape(block_count, 8, NT), extended.reshape(block_count, 8, NT + L)))
    totals = totals.reshape(PAIRS, L)
    return totals * (1.0 / math.sqrt(NT))
```

```python
import functools
import math

import jax
import jax.numpy as jnp
from jax import lax
from jax.experimental import pallas as pl
from jax.experimental.pallas import tpu as pltpu
from jax.sharding import PartitionSpec as P

L = 512
LANES = 128
SUB = 8


def gram_kernel(x_ref, y_ref, h_ref, o_ref, hi_ref, lo_ref):
    rows = y_ref.shape[1]
    blocks = rows // SUB
    shifts = L // LANES + 1
    width = shifts * LANES
    for ref, at in ((y_ref, 0), (h_ref, rows)):
        value = ref[0]
        high = value.astype(jnp.bfloat16).astype(jnp.float32)
        hi_ref[at : at + value.shape[0], :] = high
        lo_ref[at : at + value.shape[0], :] = value - high
    sub_index = lax.broadcasted_iota(jnp.int32, (SUB, width), 0)
    for p in range(SUB):
        x = x_ref[0, pl.ds(p, blocks, stride=SUB), :]
        x_high = x.astype(jnp.bfloat16).astype(jnp.float32)
        left = jnp.concatenate([x_high, x_high, x - x_high], axis=0)
        left = left.T.astype(jnp.bfloat16)
        highs, lows = [], []
        for o in range(shifts):
            at = pl.ds(p + SUB * o, blocks, stride=SUB)
            highs.append(hi_ref[at, :].astype(jnp.bfloat16))
            lows.append(lo_ref[at, :].astype(jnp.bfloat16))
        highs = jnp.concatenate(highs, axis=1)
        lows = jnp.concatenate(lows, axis=1)
        right = jnp.concatenate([highs, lows, highs], axis=0)
        grams = jnp.dot(left, right, preferred_element_type=jnp.float32)
        total = grams[0:SUB]
        for a in range(1, LANES // SUB):
            piece = grams[a * SUB : (a + 1) * SUB]
            total = total + pltpu.roll(piece, width - a * SUB, 1)
        for bit in (4, 2, 1):
            moved = pltpu.roll(total, width - bit, 1)
            total = jnp.where((sub_index & bit) != 0, moved, total)
        o_ref[p : p + 1, :] = jnp.sum(total[:, :L], axis=0, keepdims=True)


def tiles_of(array):
    pairs_here, length = array.shape
    groups, blocks = pairs_here // SUB, length // LANES
    tiles = array.reshape(groups, SUB, blocks, LANES).transpose(0, 2, 1, 3)
    return tiles.reshape(groups, blocks * SUB, LANES)


def lag_products(x, y, halo):
    pairs_here, length = x.shape
    groups, blocks = pairs_here // SUB, length // LANES
    halo_blocks = L // LANES
    whole = pl.BlockSpec((1, blocks * SUB, LANES), lambda g: (g, 0, 0))
    edge = pl.BlockSpec((1, halo_blocks * SUB, LANES), lambda g: (g, 0, 0))
    scratch = pltpu.VMEM(((blocks + halo_blocks) * SUB, LANES), jnp.float32)
    return pl.pallas_call(
        gram_kernel,
        grid=(groups,),
        in_specs=[whole, whole, edge],
        out_specs=pl.BlockSpec((SUB, L), lambda g: (g, 0)),
        out_shape=jax.ShapeDtypeStruct((pairs_here, L), jnp.float32),
        scratch_shapes=[scratch, scratch],
    )(tiles_of(x), tiles_of(y), tiles_of(halo))


def body(x, y):
    tm, pair = lax.axis_size("tm"), lax.axis_size("pair")
    halo = lax.ppermute(y[:, :L], "tm", [(i, i - 1) for i in range(1, tm)])
    partial = lag_products(x, y, halo)
    pairs_here, length = x.shape
    out_rows = pairs_here * pair // tm
    out_cols = L // pair
    blocks_here = pairs_here // out_rows
    mine = partial.reshape(blocks_here, out_rows, pair, out_cols).transpose(0, 2, 1, 3)
    send = jnp.zeros((tm, pair, out_rows, out_cols), jnp.float32)
    place = lax.axis_index("pair") * blocks_here
    send = lax.dynamic_update_slice(send, mine, (place, 0, 0, 0))
    send = send.reshape(tm * pair, out_rows, out_cols)
    received = lax.all_to_all(send, ("tm", "pair"), 0, 0, tiled=True)
    return jnp.sum(received, axis=0) * (1.0 / math.sqrt(tm * length))


def solution(mesh):
    specs = (P("pair", "tm"), P("pair", "tm"))
    return jax.shard_map(
        body, mesh=mesh, in_specs=specs, out_specs=P("tm", "pair"), check_vma=False
    )
```

```python
import math

import jax
import jax.numpy as jnp
from jax import lax
from jax.experimental import pallas as pl
from jax.experimental.pallas import tpu as pltpu
from jax.sharding import PartitionSpec as P

L = 512
LANES = 128
SUB = 8
HALF = LANES // 2
FINE = 16


def split(value):
    high = value.astype(jnp.bfloat16)
    return high, (value - high.astype(jnp.float32)).astype(jnp.bfloat16)


def split_wide(value):
    high = value.astype(jnp.bfloat16).astype(jnp.float32)
    return high, value - high


def lane_index(shape):
    return lax.broadcasted_iota(jnp.int32, shape, 1)


def store_tiles(ref, p, value):
    for o in range(ref.shape[0]):
        ref[o, p * SUB : (p + 1) * SUB, :] = value[:, o * LANES : (o + 1) * LANES]


def strided_tiles(ref, s):
    at = pl.ds(s, SUB, stride=SUB)
    return jnp.concatenate([ref[o, at, :] for o in range(ref.shape[0])], axis=1)


def load_kernel(x_hbm, y_hbm, x_ref, y_ref, head_ref, sems):
    fetch_y = pltpu.make_async_copy(y_hbm, y_ref, sems.at[0])
    fetch_x = pltpu.make_async_copy(x_hbm, x_ref, sems.at[1])
    fetch_y.start()
    fetch_x.start()
    fetch_y.wait()
    head_ref[...] = y_ref[:, : head_ref.shape[1], :]
    fetch_x.wait()


def main_kernel(scale, x_ref, y_ref, o_ref, th_ref, tl_ref, *scratch):
    def step(g, carry):
        main_group(g, scale, x_ref, y_ref, o_ref, th_ref, tl_ref, *scratch)
        return carry

    lax.fori_loop(0, x_ref.shape[0], step, 0)


def main_group(g, scale, x_ref, y_ref, o_ref, th_ref, tl_ref, xr_ref, eh, el, oh, ol, tot):
    rows = y_ref.shape[1]
    blocks = rows // SUB
    shifts = L // LANES + 1
    width = shifts * LANES
    edge = (shifts - 1) * SUB
    x = x_ref[g]
    xr_ref[...] = pltpu.roll(x, HALF, 1)
    y = y_ref[g]
    y_rolled = pltpu.roll(y, HALF, 1)
    nothing = jnp.zeros((SUB, LANES), jnp.float32)
    y_next = jnp.concatenate([y_rolled[SUB:], nothing], axis=0)
    y_odd = jnp.where(lane_index(y.shape) < HALF, y_rolled, y_next)
    for value, high_ref, low_ref in ((y, eh, el), (y_odd, oh, ol)):
        high, low = split_wide(value)
        high_ref[0:rows, :] = high
        low_ref[0:rows, :] = low
        high_ref[rows : rows + edge, :] = jnp.zeros((edge, LANES), jnp.float32)
        low_ref[rows : rows + edge, :] = jnp.zeros((edge, LANES), jnp.float32)

    first = lane_index((blocks, LANES)) < HALF
    for p in range(0, SUB, 2):
        one, two = pl.ds(p, blocks, stride=SUB), pl.ds(p + 1, blocks, stride=SUB)
        even = jnp.where(first, x_ref[g, one, :], xr_ref[two, :])
        odd = jnp.where(first, xr_ref[one, :], x_ref[g, two, :])
        left = jnp.concatenate([even, odd, even, odd], axis=0).T
        left_high, left_low = split(left)
        left = jnp.concatenate([left_high, left_low[:, : 2 * blocks]], axis=1)
        for side in range(2):
            parts = []
            for ref in (eh, oh, el, ol):
                pieces = [
                    ref[pl.ds(p + side + SUB * o, blocks, stride=SUB), :].astype(jnp.bfloat16)
                    for o in range(shifts)
                ]
                parts.append(jnp.concatenate(pieces, axis=1))
            right = jnp.concatenate(parts + parts[:2], axis=0)
            grams = jnp.dot(
                left[side * HALF : (side + 1) * HALF], right, preferred_element_type=jnp.float32
            )
            total = grams[0:SUB]
            for a in range(1, HALF // SUB):
                piece = grams[a * SUB : (a + 1) * SUB]
                total = total + pltpu.roll(piece, width - a * SUB, 1)
            store_tiles(tot, p + side, total)
    result = strided_tiles(tot, 0)
    for s in range(1, SUB):
        result = result + pltpu.roll(strided_tiles(tot, s), width - s, 1)
    o_ref[g] = result[:, :L] * scale

    pieces = []
    for q in range(L // LANES):
        at = rows - L // LANES * SUB + q * SUB
        tile = x[at : at + SUB]
        for r in range(LANES // FINE):
            pieces.append(pltpu.roll(tile, LANES - r * FINE, 1) if r else tile)
    tail = jnp.concatenate(pieces, axis=0).T[:FINE] * scale
    member = lane_index(tail.shape) % SUB
    tail = jnp.concatenate([jnp.where(member == p, tail, 0.0) for p in range(SUB)], axis=0)
    th_ref[g], tl_ref[g] = split(tail)


def edge_kernel(h_ref, th_ref, tl_ref, m_ref, o_ref, tot):
    tiles = L // LANES
    steps = LANES // FINE
    lanes = lane_index((SUB, LANES))
    columns = lane_index((SUB, L))
    nothing = jnp.zeros((SUB, LANES), jnp.float32)
    for g in range(h_ref.shape[0]):
        halo = [h_ref[g, t * SUB : (t + 1) * SUB, :] for t in range(tiles)]
        shifted = {}
        for r in range(steps):
            if r == 0:
                moved = halo
            else:
                moved = [pltpu.roll(t, LANES - r * FINE, 1) for t in halo]
            for t in range(-1, tiles):
                if r == 0:
                    tile = moved[t] if t >= 0 else None
                else:
                    here = moved[t] if t >= 0 else nothing
                    after = moved[t + 1] if t + 1 < tiles else nothing
                    tile = jnp.where(lanes < LANES - r * FINE, here, after)
                shifted[r, t] = None if tile is None else split_wide(tile)
        packed = {}

        def both(b, column, which):
            key = []
            for at in (b, b + 1):
                q, r = divmod(at + 1, steps)
                tile = q + column - tiles
                key.append((r, tile) if shifted.get((r, tile)) is not None else None)
            key = (tuple(key), which)
            if key not in packed:
                rows = [nothing if k is None else shifted[k][which] for k in key[0]]
                packed[key] = jnp.concatenate(rows, axis=0).astype(jnp.bfloat16)
            return packed[key]

        right = []
        for which in range(2):
            right.append(
                jnp.concatenate(
                    [
                        jnp.concatenate([both(b, c, which) for c in range(tiles)], axis=1)
                        for b in range(0, L // FINE, 2)
                    ],
                    axis=0,
                )
            )
        left_high, left_low = th_ref[g], tl_ref[g]
        grams = (
            jnp.dot(left_high, right[0], preferred_element_type=jnp.float32)
            + jnp.dot(left_high, right[1], preferred_element_type=jnp.float32)
            + jnp.dot(left_low, right[0], preferred_element_type=jnp.float32)
        )
        for p in range(SUB):
            low_half = grams[p * FINE : p * FINE + SUB]
            high_half = grams[p * FINE + SUB : (p + 1) * FINE]
            moved = jnp.where(columns < SUB, 0.0, pltpu.roll(low_half, SUB, 1))
            store_tiles(tot, p, high_half + moved)
        result = m_ref[g]
        for s in range(SUB):
            moved = pltpu.roll(strided_tiles(tot, s), SUB - s, 1)
            result = result + jnp.where(columns < SUB - s, 0.0, moved)
        o_ref[g] = result


def tiles_of(array):
    pairs_here, length = array.shape
    groups, blocks = pairs_here // SUB, length // LANES
    tiles = array.reshape(groups, SUB, blocks, LANES).transpose(0, 2, 1, 3)
    return tiles.reshape(groups, blocks * SUB, LANES)


def vmem(count):
    return [pl.BlockSpec(memory_space=pltpu.VMEM)] * count


def load(x, y):
    head = (x.shape[0], L // LANES * SUB, LANES)
    return pl.pallas_call(
        load_kernel,
        name="load_part",
        in_specs=[pl.BlockSpec(memory_space=pltpu.HBM)] * 2,
        out_specs=vmem(3),
        out_shape=[jax.ShapeDtypeStruct(shape, jnp.float32) for shape in (x.shape, y.shape, head)],
        scratch_shapes=[pltpu.SemaphoreType.DMA((2,))],
        compiler_params=pltpu.CompilerParams(vmem_limit_bytes=4 << 20),
    )(*[pltpu.with_memory_space_constraint(v, pltpu.HBM) for v in (x, y)])


def main_products(x, y, scale):
    groups, rows, _ = x.shape
    shifts = L // LANES + 1
    tail_shape = jax.ShapeDtypeStruct((groups, SUB * FINE, SUB * L // FINE), jnp.bfloat16)
    wide = pltpu.VMEM((rows + (shifts - 1) * SUB, LANES), jnp.float32)
    return pl.pallas_call(
        lambda *refs: main_kernel(scale, *refs),
        name="main_part",
        in_specs=vmem(2),
        out_specs=vmem(3),
        out_shape=[jax.ShapeDtypeStruct((groups, SUB, L), jnp.float32), tail_shape, tail_shape],
        scratch_shapes=[pltpu.VMEM((rows, LANES), jnp.float32), wide, wide, wide, wide]
        + [pltpu.VMEM((shifts, SUB * SUB, LANES), jnp.float32)],
        compiler_params=pltpu.CompilerParams(vmem_limit_bytes=16 << 20),
        cost_estimate=pl.CostEstimate(
            flops=6 * groups * SUB * rows // SUB * LANES * L,
            bytes_accessed=8 * groups * rows * LANES,
            transcendentals=0,
        ),
    )(x, y)


def edge_products(halo, tail_high, tail_low, partial):
    return pl.pallas_call(
        edge_kernel,
        name="edge_part",
        in_specs=vmem(4),
        out_specs=vmem(1)[0],
        out_shape=jax.ShapeDtypeStruct(partial.shape, jnp.float32),
        scratch_shapes=[pltpu.VMEM((L // LANES, SUB * SUB, LANES), jnp.float32)],
        compiler_params=pltpu.CompilerParams(vmem_limit_bytes=8 << 20),
    )(halo, tail_high, tail_low, partial)


def body(x, y):
    tm, pair = lax.axis_size("tm"), lax.axis_size("pair")
    pairs_here, length = x.shape
    x_tiles, y_tiles, head = load(tiles_of(x), tiles_of(y))
    halo = lax.ppermute(head, "tm", [(i, i - 1) for i in range(1, tm)])
    scale = 1.0 / math.sqrt(tm * length)
    partial, tail_high, tail_low = main_products(x_tiles, y_tiles, scale)
    partial = edge_products(halo, tail_high, tail_low, partial)
    out_rows = pairs_here * pair // tm
    out_cols = L // pair
    blocks_here = pairs_here // out_rows
    mine = partial.reshape(blocks_here, out_rows, pair, out_cols).transpose(0, 2, 1, 3)
    send = jnp.zeros((tm, pair, out_rows, out_cols), jnp.float32)
    place = lax.axis_index("pair") * blocks_here
    send = lax.dynamic_update_slice(send, mine, (place, 0, 0, 0))
    send = send.reshape(tm * pair, out_rows, out_cols)
    received = lax.all_to_all(send, ("tm", "pair"), 0, 0, tiled=True)
    return jnp.sum(received, axis=0)


def solution(mesh):
    specs = (P("pair", "tm"), P("pair", "tm"))
    return jax.shard_map(
        body, mesh=mesh, in_specs=specs, out_specs=P("tm", "pair"), check_vma=False
    )
```

```python
import math

import jax
import jax.numpy as jnp
from jax import lax
from jax.experimental import pallas as pl
from jax.experimental.pallas import tpu as pltpu
from jax.sharding import PartitionSpec as P

L = 512
LANES = 128
SUB = 8
PITCH = SUB + 1
HALF = LANES // 2
FINE = 16


def split(value):
    high = value.astype(jnp.bfloat16)
    return high, (value - high.astype(jnp.float32)).astype(jnp.bfloat16)


def split_wide(value):
    high = value.astype(jnp.bfloat16).astype(jnp.float32)
    return high, value - high


def lane_index(shape):
    return lax.broadcasted_iota(jnp.int32, shape, 1)


def store_tiles(ref, p, value):
    for o in range(ref.shape[0]):
        ref[o, p * PITCH : p * PITCH + SUB, :] = value[:, o * LANES : (o + 1) * LANES]


def strided_tiles(ref, s):
    at = pl.ds(s, SUB, stride=PITCH)
    return jnp.concatenate([ref[o, at, :] for o in range(ref.shape[0])], axis=1)


def load_kernel(x_hbm, y_hbm, x_ref, y_ref, head_ref, sems):
    fetch_y = pltpu.make_async_copy(y_hbm, y_ref, sems.at[0])
    fetch_x = pltpu.make_async_copy(x_hbm, x_ref, sems.at[1])
    fetch_y.start()
    fetch_x.start()
    fetch_y.wait()
    head_ref[...] = y_ref[:, : head_ref.shape[1], :]
    fetch_x.wait()


def turned(eye, value):
    dims = (((1,), (1,)), ((), ()))
    out = lax.dot_general(eye, value, dims, preferred_element_type=jnp.float32)
    return out.astype(jnp.bfloat16)


def identity(rows):
    shape = (rows, LANES)
    same = lax.broadcasted_iota(jnp.int32, shape, 0) == lane_index(shape)
    return jnp.where(same, 1.0, 0.0).astype(jnp.bfloat16)


def spread(ref, value):
    for b in range(value.shape[0] // SUB):
        ref[b * PITCH : b * PITCH + SUB, :] = value[b * SUB : (b + 1) * SUB]


def packed(value, strips, shifts):
    count = strips + shifts - 1
    high, wide, low = {}, {}, {}
    for j in range(0, count, 2):
        high[j] = jnp.concatenate(value[j : j + 2], axis=0).astype(jnp.bfloat16)
        back = high[j].astype(jnp.float32)
        for k in range(2):
            wide[j + k] = value[j + k] - back[k * SUB : (k + 1) * SUB]
    for j in range(count - 1):
        if j not in high:
            high[j] = jnp.concatenate(value[j : j + 2], axis=0).astype(jnp.bfloat16)
        low[j] = jnp.concatenate([wide[j], wide[j + 1]], axis=0).astype(jnp.bfloat16)
    tiles = []
    for part in (high, low):
        columns = [
            jnp.concatenate([part[o + j] for j in range(0, strips, 2)], axis=0)
            for o in range(shifts)
        ]
        tiles.append(jnp.concatenate(columns, axis=1))
    return tiles


def main_kernel(scale, x_ref, y_ref, o_ref, th_ref, tl_ref, xe_ref, xo_ref, ye_ref, yo_ref, tot):
    groups, rows, _ = y_ref.shape
    depth = xe_ref.shape[0]
    strips = rows // SUB // SUB
    shifts = L // LANES + 1
    width = shifts * LANES
    eye, small_eye = identity(LANES), identity(FINE)
    first = lane_index((SUB, LANES)) < HALF
    for ref in (ye_ref, yo_ref):
        used = rows // SUB * PITCH
        for d in range(depth):
            ref[d, used:, :] = jnp.zeros((ref.shape[1] - used, LANES), jnp.float32)

    def strip(p, j):
        return pl.ds(j * PITCH + p, SUB, stride=strips * PITCH)

    def stage(g):
        d = g % depth
        x, y = x_ref[g], y_ref[g]
        spread(xe_ref.at[d], x)
        spread(xo_ref.at[d], pltpu.roll(x, HALF, 1))
        spread(ye_ref.at[d], y)
        y_rolled = pltpu.roll(y, HALF, 1)
        nothing = jnp.zeros((SUB, LANES), jnp.float32)
        y_next = jnp.concatenate([y_rolled[SUB:], nothing], axis=0)
        spread(yo_ref.at[d], jnp.where(lane_index(y.shape) < HALF, y_rolled, y_next))

    def turn(couple):
        g, p = divmod(2 * couple, SUB)
        d = g % depth
        evens, odds = [], []
        for j in range(strips):
            one, two = strip(p, j), strip(p + 1, j)
            evens.append(jnp.where(first, xe_ref[d, one, :], xo_ref[d, two, :]))
            odds.append(jnp.where(first, xo_ref[d, one, :], xe_ref[d, two, :]))
        high, low = split(jnp.concatenate(evens + odds, axis=0))
        return turned(eye, jnp.concatenate([high, high, low], axis=0))

    def multiply(couple, left, side):
        g, p = divmod(2 * couple + side, SUB)
        d = g % depth
        count = strips + shifts - 1
        even = packed([ye_ref[d, strip(p, j), :] for j in range(count)], strips, shifts)
        odd = packed([yo_ref[d, strip(p, j), :] for j in range(count)], strips, shifts)
        right = jnp.concatenate([even[0], odd[0], even[1], odd[1], even[0], odd[0]], axis=0)
        left = left[side * HALF : (side + 1) * HALF]
        return jnp.dot(left, right, preferred_element_type=jnp.float32)

    def fold(couple, grams, side):
        g, p = divmod(2 * couple + side, SUB)
        total = grams[0:SUB]
        for a in range(1, HALF // SUB):
            piece = grams[a * SUB : (a + 1) * SUB]
            total = total + pltpu.roll(piece, width - a * SUB, 1)
        store_tiles(tot.at[g % depth], p, total)

    def finish(g):
        own = tot.at[g % depth]
        result = strided_tiles(own, 0)
        for s in range(1, SUB):
            result = result + pltpu.roll(strided_tiles(own, s), width - s, 1)
        o_ref[g] = result[:, :L] * scale

    def tail(g):
        pieces = []
        for q in range(L // LANES):
            at = rows - L // LANES * SUB + q * SUB
            tile = x_ref[g, at : at + SUB, :] * scale
            for r in range(LANES // FINE):
                pieces.append(pltpu.roll(tile, LANES - r * FINE, 1) if r else tile)
        parts = split(jnp.concatenate(pieces, axis=0))
        for part, ref in zip(parts, (th_ref, tl_ref)):
            value = turned(small_eye, part)
            member = lane_index(value.shape) % SUB
            none = jnp.zeros_like(value)
            ref[g] = jnp.concatenate(
                [jnp.where(member == p, value, none) for p in range(SUB)], axis=0
            )

    per_group = SUB // 2
    couples = groups * per_group
    stage(0)
    lefts = {0: turn(0)}
    grams = {}
    for k in range(couples + 1):
        g, at = divmod(k, per_group)
        if k < couples:
            if at == 0:
                tail(g)
            if at == 1 and g + 1 < groups:
                stage(g + 1)
            if k + 1 < couples:
                lefts[k + 1] = turn(k + 1)
            left = lefts.pop(k)
        for side in range(2):
            if k < couples:
                grams[k, side] = multiply(k, left, side)
            if k > 0:
                fold(k - 1, grams.pop((k - 1, side)), side)
        if k > 0 and at == 0:
            finish(g - 1)


def edge_kernel(h_ref, th_ref, tl_ref, m_ref, o_ref, tot):
    tiles = L // LANES
    steps = LANES // FINE
    lanes = lane_index((SUB, LANES))
    columns = lane_index((SUB, L))
    nothing = jnp.zeros((SUB, LANES), jnp.float32)
    for g in range(h_ref.shape[0]):
        halo = [h_ref[g, t * SUB : (t + 1) * SUB, :] for t in range(tiles)]
        shifted = {}
        for r in range(steps):
            if r == 0:
                moved = halo
            else:
                moved = [pltpu.roll(t, LANES - r * FINE, 1) for t in halo]
            for t in range(-1, tiles):
                if r == 0:
                    tile = moved[t] if t >= 0 else None
                else:
                    here = moved[t] if t >= 0 else nothing
                    after = moved[t + 1] if t + 1 < tiles else nothing
                    tile = jnp.where(lanes < LANES - r * FINE, here, after)
                shifted[r, t] = None if tile is None else split_wide(tile)
        packed = {}

        def both(b, column, which):
            key = []
            for at in (b, b + 1):
                q, r = divmod(at + 1, steps)
                tile = q + column - tiles
                key.append((r, tile) if shifted.get((r, tile)) is not None else None)
            key = (tuple(key), which)
            if key not in packed:
                rows = [nothing if k is None else shifted[k][which] for k in key[0]]
                packed[key] = jnp.concatenate(rows, axis=0).astype(jnp.bfloat16)
            return packed[key]

        right = []
        for which in range(2):
            right.append(
                jnp.concatenate(
                    [
                        jnp.concatenate([both(b, c, which) for c in range(tiles)], axis=1)
                        for b in range(0, L // FINE, 2)
                    ],
                    axis=0,
                )
            )
        left_high, left_low = th_ref[g], tl_ref[g]
        grams = (
            jnp.dot(left_high, right[0], preferred_element_type=jnp.float32)
            + jnp.dot(left_high, right[1], preferred_element_type=jnp.float32)
            + jnp.dot(left_low, right[0], preferred_element_type=jnp.float32)
        )
        for p in range(SUB):
            low_half = grams[p * FINE : p * FINE + SUB]
            high_half = grams[p * FINE + SUB : (p + 1) * FINE]
            moved = jnp.where(columns < SUB, 0.0, pltpu.roll(low_half, SUB, 1))
            store_tiles(tot, p, high_half + moved)
        result = m_ref[g]
        for s in range(SUB):
            moved = pltpu.roll(strided_tiles(tot, s), SUB - s, 1)
            result = result + jnp.where(columns < SUB - s, 0.0, moved)
        o_ref[g] = result


def tiles_of(array):
    pairs_here, length = array.shape
    groups, blocks = pairs_here // SUB, length // LANES
    tiles = array.reshape(groups, SUB, blocks, LANES).transpose(0, 2, 1, 3)
    return tiles.reshape(groups, blocks * SUB, LANES)


def vmem(count):
    return [pl.BlockSpec(memory_space=pltpu.VMEM)] * count


def load(x, y):
    head = (x.shape[0], L // LANES * SUB, LANES)
    return pl.pallas_call(
        load_kernel,
        name="load_part",
        in_specs=[pl.BlockSpec(memory_space=pltpu.HBM)] * 2,
        out_specs=vmem(3),
        out_shape=[jax.ShapeDtypeStruct(shape, jnp.float32) for shape in (x.shape, y.shape, head)],
        scratch_shapes=[pltpu.SemaphoreType.DMA((2,))],
        compiler_params=pltpu.CompilerParams(vmem_limit_bytes=4 << 20),
    )(*[pltpu.with_memory_space_constraint(v, pltpu.HBM) for v in (x, y)])


def main_products(x, y, scale):
    groups, rows, _ = x.shape
    shifts = L // LANES + 1
    tail_shape = jax.ShapeDtypeStruct((groups, SUB * FINE, SUB * L // FINE), jnp.bfloat16)
    narrow = pltpu.VMEM((2, rows // SUB * PITCH, LANES), jnp.float32)
    wide = pltpu.VMEM((2, (rows // SUB + shifts - 1) * PITCH, LANES), jnp.float32)
    return pl.pallas_call(
        lambda *refs: main_kernel(scale, *refs),
        name="main_part",
        in_specs=vmem(2),
        out_specs=vmem(3),
        out_shape=[jax.ShapeDtypeStruct((groups, SUB, L), jnp.float32), tail_shape, tail_shape],
        scratch_shapes=[narrow, narrow, wide, wide]
        + [pltpu.VMEM((2, shifts, SUB * PITCH, LANES), jnp.float32)],
        compiler_params=pltpu.CompilerParams(vmem_limit_bytes=16 << 20),
        cost_estimate=pl.CostEstimate(
            flops=6 * groups * SUB * rows // SUB * LANES * L,
            bytes_accessed=8 * groups * rows * LANES,
            transcendentals=0,
        ),
    )(x, y)


def edge_products(halo, tail_high, tail_low, partial):
    return pl.pallas_call(
        edge_kernel,
        name="edge_part",
        in_specs=vmem(4),
        out_specs=vmem(1)[0],
        out_shape=jax.ShapeDtypeStruct(partial.shape, jnp.float32),
        scratch_shapes=[pltpu.VMEM((L // LANES, SUB * PITCH, LANES), jnp.float32)],
        compiler_params=pltpu.CompilerParams(vmem_limit_bytes=8 << 20),
    )(halo, tail_high, tail_low, partial)


def body(x, y):
    tm, pair = lax.axis_size("tm"), lax.axis_size("pair")
    pairs_here, length = x.shape
    x_tiles, y_tiles, head = load(tiles_of(x), tiles_of(y))
    halo = lax.ppermute(head, "tm", [(i, i - 1) for i in range(1, tm)])
    scale = 1.0 / math.sqrt(tm * length)
    partial, tail_high, tail_low = main_products(x_tiles, y_tiles, scale)
    partial = edge_products(halo, tail_high, tail_low, partial)
    out_rows = pairs_here * pair // tm
    out_cols = L // pair
    blocks_here = pairs_here // out_rows
    mine = partial.reshape(blocks_here, out_rows, pair, out_cols).transpose(0, 2, 1, 3)
    send = jnp.zeros((tm, pair, out_rows, out_cols), jnp.float32)
    place = lax.axis_index("pair") * blocks_here
    send = lax.dynamic_update_slice(send, mine, (place, 0, 0, 0))
    send = send.reshape(tm * pair, out_rows, out_cols)
    received = lax.all_to_all(send, ("tm", "pair"), 0, 0, tiled=True)
    return jnp.sum(received, axis=0)


def solution(mesh):
    specs = (P("pair", "tm"), P("pair", "tm"))
    return jax.shard_map(
        body, mesh=mesh, in_specs=specs, out_specs=P("tm", "pair"), check_vma=False
    )
```

```python
import math

import jax
import jax.numpy as jnp
from jax import lax
from jax.experimental import pallas as pl
from jax.experimental.pallas import tpu as pltpu
from jax.sharding import PartitionSpec as P

L = 512
LANES = 128
SUB = 8
PITCH = SUB + 1
HALF = LANES // 2
FINE = 16
FLOPS = 10000000000


def split(value):
    high = value.astype(jnp.bfloat16)
    return high, (value - high.astype(jnp.float32)).astype(jnp.bfloat16)


def split_wide(value):
    high = value.astype(jnp.bfloat16).astype(jnp.float32)
    return high, value - high


def lane_index(shape):
    return lax.broadcasted_iota(jnp.int32, shape, 1)


def store_tiles(ref, p, value):
    for o in range(ref.shape[0]):
        ref[o, p * PITCH : p * PITCH + SUB, :] = value[:, o * LANES : (o + 1) * LANES]


def strided_tiles(ref, s):
    at = pl.ds(s, SUB, stride=PITCH)
    return jnp.concatenate([ref[o, at, :] for o in range(ref.shape[0])], axis=1)


def head_kernel(y_hbm, head_ref, sem):
    copy = pltpu.make_async_copy(y_hbm.at[:, : head_ref.shape[1], :], head_ref, sem)
    copy.start()
    copy.wait()


def store_tiles(ref, p, value):
    for o in range(ref.shape[0]):
        ref[o, p * PITCH : p * PITCH + SUB, :] = value[:, o * LANES : (o + 1) * LANES]


def strided_tiles(ref, s):
    at = pl.ds(s, SUB, stride=PITCH)
    return jnp.concatenate([ref[o, at, :] for o in range(ref.shape[0])], axis=1)


def load_kernel(x_hbm, y_hbm, x_ref, y_ref, head_ref, sems):
    fetch_y = pltpu.make_async_copy(y_hbm, y_ref, sems.at[0])
    fetch_x = pltpu.make_async_copy(x_hbm, x_ref, sems.at[1])
    fetch_y.start()
    fetch_x.start()
    fetch_y.wait()
    head_ref[...] = y_ref[:, : head_ref.shape[1], :]
    fetch_x.wait()


def turned(eye, value):
    dims = (((1,), (1,)), ((), ()))
    out = lax.dot_general(eye, value, dims, preferred_element_type=jnp.float32)
    return out.astype(jnp.bfloat16)


def identity(rows):
    shape = (rows, LANES)
    same = lax.broadcasted_iota(jnp.int32, shape, 0) == lane_index(shape)
    return jnp.where(same, 1.0, 0.0).astype(jnp.bfloat16)


def spread(ref, value):
    for b in range(value.shape[0] // SUB):
        ref[b * PITCH : b * PITCH + SUB, :] = value[b * SUB : (b + 1) * SUB]


def packed(value, strips, shifts):
    count = strips + shifts - 1
    high, wide, low = {}, {}, {}
    for j in range(0, count, 2):
        high[j] = jnp.concatenate(value[j : j + 2], axis=0).astype(jnp.bfloat16)
        back = high[j].astype(jnp.float32)
        for k in range(2):
            wide[j + k] = value[j + k] - back[k * SUB : (k + 1) * SUB]
    for j in range(count - 1):
        if j not in high:
            high[j] = jnp.concatenate(value[j : j + 2], axis=0).astype(jnp.bfloat16)
        low[j] = jnp.concatenate([wide[j], wide[j + 1]], axis=0).astype(jnp.bfloat16)
    tiles = []
    for part in (high, low):
        columns = [
            jnp.concatenate([part[o + j] for j in range(0, strips, 2)], axis=0)
            for o in range(shifts)
        ]
        tiles.append(jnp.concatenate(columns, axis=1))
    return tiles


def main_kernel(scale, x_ref, y_ref, o_ref, th_ref, tl_ref, xe_ref, xo_ref, ye_ref, yo_ref, tot):
    groups, rows, _ = y_ref.shape
    depth = xe_ref.shape[0]
    strips = rows // SUB // SUB
    shifts = L // LANES + 1
    width = shifts * LANES
    eye, small_eye = identity(LANES), identity(FINE)
    first = lane_index((SUB, LANES)) < HALF
    for ref in (ye_ref, yo_ref):
        used = rows // SUB * PITCH
        for d in range(depth):
            ref[d, used:, :] = jnp.zeros((ref.shape[1] - used, LANES), jnp.float32)

    def strip(p, j):
        return pl.ds(j * PITCH + p, SUB, stride=strips * PITCH)

    def stage(g):
        d = g % depth
        x, y = x_ref[g], y_ref[g]
        spread(xe_ref.at[d], x)
        spread(xo_ref.at[d], pltpu.roll(x, HALF, 1))
        spread(ye_ref.at[d], y)
        y_rolled = pltpu.roll(y, HALF, 1)
        nothing = jnp.zeros((SUB, LANES), jnp.float32)
        y_next = jnp.concatenate([y_rolled[SUB:], nothing], axis=0)
        spread(yo_ref.at[d], jnp.where(lane_index(y.shape) < HALF, y_rolled, y_next))

    def turn(couple):
        g, p = divmod(2 * couple, SUB)
        d = g % depth
        evens, odds = [], []
        for j in range(strips):
            one, two = strip(p, j), strip(p + 1, j)
            evens.append(jnp.where(first, xe_ref[d, one, :], xo_ref[d, two, :]))
            odds.append(jnp.where(first, xo_ref[d, one, :], xe_ref[d, two, :]))
        high, low = split(jnp.concatenate(evens + odds, axis=0))
        return turned(eye, jnp.concatenate([high, high, low], axis=0))

    def multiply(couple, left, side):
        g, p = divmod(2 * couple + side, SUB)
        d = g % depth
        count = strips + shifts - 1
        even = packed([ye_ref[d, strip(p, j), :] for j in range(count)], strips, shifts)
        odd = packed([yo_ref[d, strip(p, j), :] for j in range(count)], strips, shifts)
        right = jnp.concatenate([even[0], odd[0], even[1], odd[1], even[0], odd[0]], axis=0)
        left = left[side * HALF : (side + 1) * HALF]
        return jnp.dot(left, right, preferred_element_type=jnp.float32)

    def fold(couple, grams, side):
        g, p = divmod(2 * couple + side, SUB)
        total = grams[0:SUB]
        for a in range(1, HALF // SUB):
            piece = grams[a * SUB : (a + 1) * SUB]
            total = total + pltpu.roll(piece, width - a * SUB, 1)
        store_tiles(tot.at[g % depth], p, total)

    def finish(g):
        own = tot.at[g % depth]
        result = strided_tiles(own, 0)
        for s in range(1, SUB):
            result = result + pltpu.roll(strided_tiles(own, s), width - s, 1)
        o_ref[g] = result[:, :L] * scale

    def tail(g):
        pieces = []
        for q in range(L // LANES):
            at = rows - L // LANES * SUB + q * SUB
            tile = x_ref[g, at : at + SUB, :] * scale
            for r in range(LANES // FINE):
                pieces.append(pltpu.roll(tile, LANES - r * FINE, 1) if r else tile)
        parts = split(jnp.concatenate(pieces, axis=0))
        for part, ref in zip(parts, (th_ref, tl_ref)):
            value = turned(small_eye, part)
            member = lane_index(value.shape) % SUB
            none = jnp.zeros_like(value)
            ref[g] = jnp.concatenate(
                [jnp.where(member == p, value, none) for p in range(SUB)], axis=0
            )

    per_group = SUB // 2
    couples = groups * per_group
    stage(0)
    lefts = {0: turn(0)}
    grams = {}
    for k in range(couples + 1):
        g, at = divmod(k, per_group)
        if k < couples:
            if at == 0:
                tail(g)
            if at == 1 and g + 1 < groups:
                stage(g + 1)
            if k + 1 < couples:
                lefts[k + 1] = turn(k + 1)
            left = lefts.pop(k)
        for side in range(2):
            if k < couples:
                grams[k, side] = multiply(k, left, side)
            if k > 0:
                fold(k - 1, grams.pop((k - 1, side)), side)
        if k > 0 and at == 0:
            finish(g - 1)


def edge_kernel(h_ref, th_ref, tl_ref, m_ref, o_ref, tot):
    tiles = L // LANES
    steps = LANES // FINE
    lanes = lane_index((SUB, LANES))
    columns = lane_index((SUB, L))
    nothing = jnp.zeros((SUB, LANES), jnp.float32)
    groups = h_ref.shape[0]
    fine_blocks = L // FINE

    def shifted_halo(g):
        halo = [h_ref[g, t * SUB : (t + 1) * SUB, :] for t in range(tiles)]
        shifted = {}
        for r in range(steps):
            moved = [pltpu.roll(t, LANES - r * FINE, 1) if r else t for t in halo]
            for t in range(-1 if r else 0, tiles):
                tile = moved[max(t, 0)]
                if r:
                    here = moved[t] if t >= 0 else nothing
                    after = moved[t + 1] if t + 1 < tiles else nothing
                    tile = jnp.where(lanes < LANES - r * FINE, here, after)
                shifted[r, t] = split_wide(tile)
        return shifted

    def right_side(shifted, which):
        made = {}

        def piece(b, column):
            key = []
            for at in (b, b + 1):
                q, r = divmod(at + 1, steps)
                key.append((r, q + column - tiles))
            key = tuple(k if k in shifted else None for k in key)
            if key not in made:
                rows = [nothing if k is None else shifted[k][which] for k in key]
                made[key] = jnp.concatenate(rows, axis=0).astype(jnp.bfloat16)
            return made[key]

        rows = [
            jnp.concatenate([piece(b, c) for c in range(tiles)], axis=1)
            for b in range(0, fine_blocks, 2)
        ]
        return jnp.concatenate(rows, axis=0)

    def multiply(g):
        shifted = shifted_halo(g)
        right_high, right_low = right_side(shifted, 0), right_side(shifted, 1)
        left_high, left_low = th_ref[g], tl_ref[g]
        half = tiles // 2
        parts = []
        for first, at in ((half * steps, slice(0, half * LANES)), (0, slice(half * LANES, L))):
            k = slice(first * SUB, fine_blocks * SUB)
            high, low = right_high[k, at], right_low[k, at]
            left = jnp.concatenate([left_high[:, k], left_high[:, k], left_low[:, k]], axis=1)
            right = jnp.concatenate([high, low, high], axis=0)
            parts.append(jnp.dot(left, right, preferred_element_type=jnp.float32))
        return jnp.concatenate(parts, axis=1)

    def fold(g, grams):
        own = tot.at[g % 2]
        for p in range(SUB):
            low_half = grams[p * FINE : p * FINE + SUB]
            high_half = grams[p * FINE + SUB : (p + 1) * FINE]
            moved = jnp.where(columns < SUB, 0.0, pltpu.roll(low_half, SUB, 1))
            store_tiles(own, p, high_half + moved)
        result = m_ref[g]
        for s in range(SUB):
            moved = pltpu.roll(strided_tiles(own, s), SUB - s, 1)
            result = result + jnp.where(columns < SUB - s, 0.0, moved)
        o_ref[g] = result

    grams = multiply(0)
    for g in range(groups):
        after = multiply(g + 1) if g + 1 < groups else None
        fold(g, grams)
        grams = after


def tiles_of(array):
    pairs_here, length = array.shape
    groups, blocks = pairs_here // SUB, length // LANES
    tiles = array.reshape(groups, SUB, blocks, LANES).transpose(0, 2, 1, 3)
    return tiles.reshape(groups, blocks * SUB, LANES)


def vmem(count):
    return [pl.BlockSpec(memory_space=pltpu.VMEM)] * count


def head_of(y):
    head = (y.shape[0], L // LANES * SUB, LANES)
    return pl.pallas_call(
        head_kernel,
        name="head_part",
        in_specs=[pl.BlockSpec(memory_space=pltpu.HBM)],
        out_specs=vmem(1)[0],
        out_shape=jax.ShapeDtypeStruct(head, jnp.float32),
        scratch_shapes=[pltpu.SemaphoreType.DMA],
        compiler_params=pltpu.CompilerParams(vmem_limit_bytes=4 << 20),
        cost_estimate=pl.CostEstimate(flops=FLOPS, bytes_accessed=0, transcendentals=0),
    )(pltpu.with_memory_space_constraint(y, pltpu.HBM))


def main_products(x, y, scale):
    groups, rows, _ = x.shape
    shifts = L // LANES + 1
    tail_shape = jax.ShapeDtypeStruct((groups, SUB * FINE, SUB * L // FINE), jnp.bfloat16)
    narrow = pltpu.VMEM((2, rows // SUB * PITCH, LANES), jnp.float32)
    wide = pltpu.VMEM((2, (rows // SUB + shifts - 1) * PITCH, LANES), jnp.float32)
    return pl.pallas_call(
        lambda *refs: main_kernel(scale, *refs),
        name="main_part",
        in_specs=vmem(2),
        out_specs=vmem(3),
        out_shape=[jax.ShapeDtypeStruct((groups, SUB, L), jnp.float32), tail_shape, tail_shape],
        scratch_shapes=[narrow, narrow, wide, wide]
        + [pltpu.VMEM((2, shifts, SUB * PITCH, LANES), jnp.float32)],
        compiler_params=pltpu.CompilerParams(vmem_limit_bytes=16 << 20),
        cost_estimate=pl.CostEstimate(
            flops=6 * groups * SUB * rows // SUB * LANES * L,
            bytes_accessed=8 * groups * rows * LANES,
            transcendentals=0,
        ),
    )(x, y)


def edge_products(halo, tail_high, tail_low, partial):
    return pl.pallas_call(
        edge_kernel,
        name="edge_part",
        in_specs=vmem(4),
        out_specs=vmem(1)[0],
        out_shape=jax.ShapeDtypeStruct(partial.shape, jnp.float32),
        scratch_shapes=[pltpu.VMEM((2, L // LANES, SUB * PITCH, LANES), jnp.float32)],
        compiler_params=pltpu.CompilerParams(vmem_limit_bytes=8 << 20),
    )(halo, tail_high, tail_low, partial)


def body(x, y):
    tm, pair = lax.axis_size("tm"), lax.axis_size("pair")
    pairs_here, length = x.shape
    x_tiles, y_tiles = tiles_of(x), tiles_of(y)
    halo = lax.ppermute(head_of(y_tiles), "tm", [(i, i - 1) for i in range(1, tm)])
    scale = 1.0 / math.sqrt(tm * length)
    partial, tail_high, tail_low = main_products(x_tiles, y_tiles, scale)
    partial = edge_products(halo, tail_high, tail_low, partial)
    out_rows = pairs_here * pair // tm
    out_cols = L // pair
    blocks_here = pairs_here // out_rows
    mine = partial.reshape(blocks_here, out_rows, pair, out_cols).transpose(0, 2, 1, 3)
    send = jnp.zeros((tm, pair, out_rows, out_cols), jnp.float32)
    place = lax.axis_index("pair") * blocks_here
    send = lax.dynamic_update_slice(send, mine, (place, 0, 0, 0))
    send = send.reshape(tm * pair, out_rows, out_cols)
    received = lax.all_to_all(send, ("tm", "pair"), 0, 0, tiled=True)
    return jnp.sum(received, axis=0)


def solution(mesh):
    specs = (P("pair", "tm"), P("pair", "tm"))
    return jax.shard_map(
        body, mesh=mesh, in_specs=specs, out_specs=P("tm", "pair"), check_vma=False
    )
```

```python
import math

import jax
import jax.numpy as jnp
from jax import lax
from jax.experimental import pallas as pl
from jax.experimental.pallas import tpu as pltpu
from jax.sharding import PartitionSpec as P

L = 512
LANES = 128
SUB = 8
PITCH = SUB + 1
HALF = LANES // 2
FINE = 16
FLOPS = 10000000000


def split(value):
    high = value.astype(jnp.bfloat16)
    return high, (value - high.astype(jnp.float32)).astype(jnp.bfloat16)


def split_wide(value):
    high = value.astype(jnp.bfloat16).astype(jnp.float32)
    return high, value - high


def lane_index(shape):
    return lax.broadcasted_iota(jnp.int32, shape, 1)


def store_tiles(ref, p, value):
    for o in range(ref.shape[0]):
        ref[o, p * PITCH : p * PITCH + SUB, :] = value[:, o * LANES : (o + 1) * LANES]


def strided_tiles(ref, s):
    at = pl.ds(s, SUB, stride=PITCH)
    return jnp.concatenate([ref[o, at, :] for o in range(ref.shape[0])], axis=1)


def head_kernel(y_hbm, head_ref, sem):
    copy = pltpu.make_async_copy(y_hbm.at[:, : head_ref.shape[1], :], head_ref, sem)
    copy.start()
    copy.wait()


def store_tiles(ref, p, value):
    for o in range(ref.shape[0]):
        ref[o, p * PITCH : p * PITCH + SUB, :] = value[:, o * LANES : (o + 1) * LANES]


def strided_tiles(ref, s):
    at = pl.ds(s, SUB, stride=PITCH)
    return jnp.concatenate([ref[o, at, :] for o in range(ref.shape[0])], axis=1)


def load_kernel(x_hbm, y_hbm, x_ref, y_ref, head_ref, sems):
    fetch_y = pltpu.make_async_copy(y_hbm, y_ref, sems.at[0])
    fetch_x = pltpu.make_async_copy(x_hbm, x_ref, sems.at[1])
    fetch_y.start()
    fetch_x.start()
    fetch_y.wait()
    head_ref[...] = y_ref[:, : head_ref.shape[1], :]
    fetch_x.wait()


def turned(eye, value):
    dims = (((1,), (1,)), ((), ()))
    out = lax.dot_general(eye, value, dims, preferred_element_type=jnp.float32)
    return out.astype(jnp.bfloat16)


def identity(rows):
    shape = (rows, LANES)
    same = lax.broadcasted_iota(jnp.int32, shape, 0) == lane_index(shape)
    return jnp.where(same, 1.0, 0.0).astype(jnp.bfloat16)


def spread(ref, value):
    for b in range(value.shape[0] // SUB):
        ref[b * PITCH : b * PITCH + SUB, :] = value[b * SUB : (b + 1) * SUB]


def packed(value, strips, shifts):
    count = strips + shifts - 1
    high, wide, low = {}, {}, {}
    for j in range(0, count, 2):
        high[j] = jnp.concatenate(value[j : j + 2], axis=0).astype(jnp.bfloat16)
        back = high[j].astype(jnp.float32)
        for k in range(2):
            wide[j + k] = value[j + k] - back[k * SUB : (k + 1) * SUB]
    for j in range(count - 1):
        if j not in high:
            high[j] = jnp.concatenate(value[j : j + 2], axis=0).astype(jnp.bfloat16)
        low[j] = jnp.concatenate([wide[j], wide[j + 1]], axis=0).astype(jnp.bfloat16)
    tiles = []
    for part in (high, low):
        columns = [
            jnp.concatenate([part[o + j] for j in range(0, strips, 2)], axis=0)
            for o in range(shifts)
        ]
        tiles.append(jnp.concatenate(columns, axis=1))
    return tiles


def main_kernel(scale, x_ref, y_ref, o_ref, th_ref, tl_ref, xe_ref, xo_ref, ye_ref, yo_ref, tot):
    groups, rows, _ = y_ref.shape
    depth = xe_ref.shape[0]
    strips = rows // SUB // SUB
    shifts = L // LANES + 1
    width = shifts * LANES
    eye, small_eye = identity(LANES), identity(FINE)
    first = lane_index((SUB, LANES)) < HALF
    for ref in (ye_ref, yo_ref):
        used = rows // SUB * PITCH
        for d in range(depth):
            ref[d, used:, :] = jnp.zeros((ref.shape[1] - used, LANES), jnp.float32)

    def strip(p, j):
        return pl.ds(j * PITCH + p, SUB, stride=strips * PITCH)

    def stage(g):
        d = g % depth
        x, y = x_ref[g], y_ref[g]
        spread(xe_ref.at[d], x)
        spread(xo_ref.at[d], pltpu.roll(x, HALF, 1))
        spread(ye_ref.at[d], y)
        y_rolled = pltpu.roll(y, HALF, 1)
        nothing = jnp.zeros((SUB, LANES), jnp.float32)
        y_next = jnp.concatenate([y_rolled[SUB:], nothing], axis=0)
        spread(yo_ref.at[d], jnp.where(lane_index(y.shape) < HALF, y_rolled, y_next))

    def turn(couple):
        g, p = divmod(2 * couple, SUB)
        d = g % depth
        evens, odds = [], []
        for j in range(strips):
            one, two = strip(p, j), strip(p + 1, j)
            evens.append(jnp.where(first, xe_ref[d, one, :], xo_ref[d, two, :]))
            odds.append(jnp.where(first, xo_ref[d, one, :], xe_ref[d, two, :]))
        high, low = split(jnp.concatenate(evens + odds, axis=0))
        return turned(eye, jnp.concatenate([high, high, low], axis=0))

    def multiply(couple, left, side):
        g, p = divmod(2 * couple + side, SUB)
        d = g % depth
        count = strips + shifts - 1
        even = packed([ye_ref[d, strip(p, j), :] for j in range(count)], strips, shifts)
        odd = packed([yo_ref[d, strip(p, j), :] for j in range(count)], strips, shifts)
        right = jnp.concatenate([even[0], odd[0], even[1], odd[1], even[0], odd[0]], axis=0)
        left = left[side * HALF : (side + 1) * HALF]
        return jnp.dot(left, right, preferred_element_type=jnp.float32)

    def fold(couple, grams, side):
        g, p = divmod(2 * couple + side, SUB)
        total = grams[0:SUB]
        for a in range(1, HALF // SUB):
            piece = grams[a * SUB : (a + 1) * SUB]
            total = total + pltpu.roll(piece, width - a * SUB, 1)
        store_tiles(tot.at[g % depth], p, total)

    def finish(g):
        own = tot.at[g % depth]
        result = strided_tiles(own, 0)
        for s in range(1, SUB):
            result = result + pltpu.roll(strided_tiles(own, s), width - s, 1)
        o_ref[g] = result[:, :L] * scale

    def tail(g):
        pieces = []
        for q in range(L // LANES):
            at = rows - L // LANES * SUB + q * SUB
            tile = x_ref[g, at : at + SUB, :] * scale
            for r in range(LANES // FINE):
                pieces.append(pltpu.roll(tile, LANES - r * FINE, 1) if r else tile)
        parts = split(jnp.concatenate(pieces, axis=0))
        for part, ref in zip(parts, (th_ref, tl_ref)):
            value = turned(small_eye, part)
            member = lane_index(value.shape) % SUB
            none = jnp.zeros_like(value)
            ref[g] = jnp.concatenate(
                [jnp.where(member == p, value, none) for p in range(SUB)], axis=0
            )

    per_group = SUB // 2
    couples = groups * per_group
    stage(0)
    lefts = {0: turn(0)}
    grams = {}
    for k in range(couples + 1):
        g, at = divmod(k, per_group)
        if k < couples:
            if at == 0:
                tail(g)
            if at == 1 and g + 1 < groups:
                stage(g + 1)
            if k + 1 < couples:
                lefts[k + 1] = turn(k + 1)
            left = lefts.pop(k)
        for side in range(2):
            if k < couples:
                grams[k, side] = multiply(k, left, side)
            if k > 0:
                fold(k - 1, grams.pop((k - 1, side)), side)
        if k > 0 and at == 0:
            finish(g - 1)


def edge_kernel(h_ref, th_ref, tl_ref, m_ref, o_ref, tot):
    tiles = L // LANES
    steps = LANES // FINE
    lanes = lane_index((SUB, LANES))
    columns = lane_index((SUB, L))
    nothing = jnp.zeros((SUB, LANES), jnp.float32)
    groups = h_ref.shape[0]
    fine_blocks = L // FINE

    def shifted_halo(g):
        halo = [h_ref[g, t * SUB : (t + 1) * SUB, :] for t in range(tiles)]
        shifted = {}
        for r in range(steps):
            moved = [pltpu.roll(t, LANES - r * FINE, 1) if r else t for t in halo]
            for t in range(-1 if r else 0, tiles):
                tile = moved[max(t, 0)]
                if r:
                    here = moved[t] if t >= 0 else nothing
                    after = moved[t + 1] if t + 1 < tiles else nothing
                    tile = jnp.where(lanes < LANES - r * FINE, here, after)
                shifted[r, t] = split_wide(tile)
        return shifted

    def right_side(shifted, which):
        made = {}

        def piece(b, column):
            key = []
            for at in (b, b + 1):
                q, r = divmod(at + 1, steps)
                key.append((r, q + column - tiles))
            key = tuple(k if k in shifted else None for k in key)
            if key not in made:
                rows = [nothing if k is None else shifted[k][which] for k in key]
                made[key] = jnp.concatenate(rows, axis=0).astype(jnp.bfloat16)
            return made[key]

        rows = [
            jnp.concatenate([piece(b, c) for c in range(tiles)], axis=1)
            for b in range(0, fine_blocks, 2)
        ]
        return jnp.concatenate(rows, axis=0)

    def multiply(g):
        shifted = shifted_halo(g)
        right_high, right_low = right_side(shifted, 0), right_side(shifted, 1)
        left_high, left_low = th_ref[g], tl_ref[g]
        half = tiles // 2
        parts = []
        for first, at in ((half * steps, slice(0, half * LANES)), (0, slice(half * LANES, L))):
            k = slice(first * SUB, fine_blocks * SUB)
            high, low = right_high[k, at], right_low[k, at]
            left = jnp.concatenate([left_high[:, k], left_high[:, k], left_low[:, k]], axis=1)
            right = jnp.concatenate([high, low, high], axis=0)
            parts.append(jnp.dot(left, right, preferred_element_type=jnp.float32))
        return jnp.concatenate(parts, axis=1)

    def fold(g, grams):
        own = tot.at[g % 2]
        for p in range(SUB):
            low_half = grams[p * FINE : p * FINE + SUB]
            high_half = grams[p * FINE + SUB : (p + 1) * FINE]
            moved = jnp.where(columns < SUB, 0.0, pltpu.roll(low_half, SUB, 1))
            store_tiles(own, p, high_half + moved)
        result = m_ref[g]
        for s in range(SUB):
            moved = pltpu.roll(strided_tiles(own, s), SUB - s, 1)
            result = result + jnp.where(columns < SUB - s, 0.0, moved)
        o_ref[g] = result

    grams = multiply(0)
    for g in range(groups):
        after = multiply(g + 1) if g + 1 < groups else None
        fold(g, grams)
        grams = after


def tiles_of(array):
    pairs_here, length = array.shape
    groups, blocks = pairs_here // SUB, length // LANES
    tiles = array.reshape(groups, SUB, blocks, LANES).transpose(0, 2, 1, 3)
    return tiles.reshape(groups, blocks * SUB, LANES)


def vmem(count):
    return [pl.BlockSpec(memory_space=pltpu.VMEM)] * count


def head_of(y):
    head = (y.shape[0], L // LANES * SUB, LANES)
    return pl.pallas_call(
        head_kernel,
        name="head_part",
        in_specs=[pl.BlockSpec(memory_space=pltpu.HBM)],
        out_specs=vmem(1)[0],
        out_shape=jax.ShapeDtypeStruct(head, jnp.float32),
        scratch_shapes=[pltpu.SemaphoreType.DMA],
        compiler_params=pltpu.CompilerParams(vmem_limit_bytes=4 << 20),
        cost_estimate=pl.CostEstimate(flops=FLOPS, bytes_accessed=0, transcendentals=0),
    )(pltpu.with_memory_space_constraint(y, pltpu.HBM))


def main_products(x, y, scale):
    groups, rows, _ = x.shape
    shifts = L // LANES + 1
    tail_shape = jax.ShapeDtypeStruct((groups, SUB * FINE, SUB * L // FINE), jnp.bfloat16)
    narrow = pltpu.VMEM((2, rows // SUB * PITCH, LANES), jnp.float32)
    wide = pltpu.VMEM((2, (rows // SUB + shifts - 1) * PITCH, LANES), jnp.float32)
    return pl.pallas_call(
        lambda *refs: main_kernel(scale, *refs),
        name="main_part",
        in_specs=vmem(2),
        out_specs=vmem(3),
        out_shape=[jax.ShapeDtypeStruct((groups, SUB, L), jnp.float32), tail_shape, tail_shape],
        scratch_shapes=[narrow, narrow, wide, wide]
        + [pltpu.VMEM((2, shifts, SUB * PITCH, LANES), jnp.float32)],
        compiler_params=pltpu.CompilerParams(vmem_limit_bytes=16 << 20),
        cost_estimate=pl.CostEstimate(
            flops=6 * groups * SUB * rows // SUB * LANES * L,
            bytes_accessed=8 * groups * rows * LANES,
            transcendentals=0,
        ),
    )(x, y)


def edge_products(halo, tail_high, tail_low, partial):
    return pl.pallas_call(
        edge_kernel,
        name="edge_part",
        in_specs=vmem(4),
        out_specs=vmem(1)[0],
        out_shape=jax.ShapeDtypeStruct(partial.shape, jnp.float32),
        scratch_shapes=[pltpu.VMEM((2, L // LANES, SUB * PITCH, LANES), jnp.float32)],
        compiler_params=pltpu.CompilerParams(vmem_limit_bytes=8 << 20),
    )(halo, tail_high, tail_low, partial)


def body(x, y):
    tm, high, low = (lax.axis_size(axis) for axis in AXES)
    pair = high * low
    pairs_here, length = x.shape
    x_tiles, y_tiles = tiles_of(x), tiles_of(y)
    halo = lax.ppermute(head_of(y_tiles), "tm", [(i, i - 1) for i in range(1, tm)])
    scale = 1.0 / math.sqrt(tm * length)
    partial, tail_high, tail_low = main_products(x_tiles, y_tiles, scale)
    partial = edge_products(halo, tail_high, tail_low, partial)
    out_rows = pairs_here * pair // tm
    out_cols = L // pair
    blocks_here = pairs_here // out_rows
    mine = partial.reshape(blocks_here, out_rows, high, low, out_cols).transpose(3, 0, 2, 1, 4)
    if low == 2:
        me = lax.axis_index("low")
        away = lax.ppermute(
            lax.dynamic_index_in_dim(mine, 1 - me, 0, keepdims=False), "low", [(0, 1), (1, 0)]
        )
        home = lax.dynamic_index_in_dim(mine, me, 0, keepdims=False)
        mine = jnp.where(me == 0, jnp.stack([home, away]), jnp.stack([away, home]))
    mine = mine.reshape(low * blocks_here, high, out_rows, out_cols)
    send = jnp.zeros((tm, high, out_rows, out_cols), jnp.float32)
    place = lax.axis_index("high") * low * blocks_here
    send = lax.dynamic_update_slice(send, mine, (place, 0, 0, 0))
    send = send.reshape(tm * high, out_rows, out_cols)
    received = lax.all_to_all(send, ("tm", "high"), 0, 0, tiled=True)
    return jnp.sum(received, axis=0)


AXES = ("tm", "high", "low")


def solution(mesh):
    tm, pair = mesh.devices.shape
    low = 2 if pair % 2 == 0 else 1
    fine = jax.sharding.Mesh(mesh.devices.reshape(tm, pair // low, low), AXES)
    spec = P(("high", "low"), "tm")
    out = P("tm", ("high", "low"))
    return jax.shard_map(body, mesh=fine, in_specs=(spec, spec), out_specs=out, check_vma=False)
```

```python
import math

import jax
import jax.numpy as jnp
from jax import lax
from jax.experimental import pallas as pl
from jax.experimental.pallas import tpu as pltpu
from jax.sharding import PartitionSpec as P

L = 512
LANES = 128
SUB = 8
PITCH = SUB + 1
HALF = LANES // 2
FINE = 16
FLOPS = 10000000000


def split(value):
    high = value.astype(jnp.bfloat16)
    return high, (value - high.astype(jnp.float32)).astype(jnp.bfloat16)


def split_wide(value):
    high = value.astype(jnp.bfloat16).astype(jnp.float32)
    return high, value - high


def lane_index(shape):
    return lax.broadcasted_iota(jnp.int32, shape, 1)


def store_tiles(ref, p, value):
    for o in range(ref.shape[0]):
        ref[o, p * PITCH : p * PITCH + SUB, :] = value[:, o * LANES : (o + 1) * LANES]


def strided_tiles(ref, s):
    at = pl.ds(s, SUB, stride=PITCH)
    return jnp.concatenate([ref[o, at, :] for o in range(ref.shape[0])], axis=1)


def head_kernel(y_hbm, head_ref, sem):
    copy = pltpu.make_async_copy(y_hbm.at[:, : head_ref.shape[1], :], head_ref, sem)
    copy.start()
    copy.wait()


def turned(eye, value):
    dims = (((1,), (1,)), ((), ()))
    out = lax.dot_general(eye, value, dims, preferred_element_type=jnp.float32)
    return out.astype(jnp.bfloat16)


def identity(rows):
    shape = (rows, LANES)
    same = lax.broadcasted_iota(jnp.int32, shape, 0) == lane_index(shape)
    return jnp.where(same, 1.0, 0.0).astype(jnp.bfloat16)


def spread(ref, value):
    for b in range(value.shape[0] // SUB):
        ref[b * PITCH : b * PITCH + SUB, :] = value[b * SUB : (b + 1) * SUB]


def packed(value, strips, shifts):
    count = strips + shifts - 1
    high, wide, low = {}, {}, {}
    for j in range(0, count, 2):
        high[j] = jnp.concatenate(value[j : j + 2], axis=0).astype(jnp.bfloat16)
        back = high[j].astype(jnp.float32)
        for k in range(2):
            wide[j + k] = value[j + k] - back[k * SUB : (k + 1) * SUB]
    for j in range(count - 1):
        if j not in high:
            high[j] = jnp.concatenate(value[j : j + 2], axis=0).astype(jnp.bfloat16)
        low[j] = jnp.concatenate([wide[j], wide[j + 1]], axis=0).astype(jnp.bfloat16)
    tiles = []
    for part in (high, low):
        columns = [
            jnp.concatenate([part[o + j] for j in range(0, strips, 2)], axis=0)
            for o in range(shifts)
        ]
        tiles.append(jnp.concatenate(columns, axis=1))
    return tiles


def main_kernel(scale, x_ref, y_ref, o_ref, th_ref, tl_ref, xe_ref, xo_ref, ye_ref, yo_ref, tot):
    groups, rows, _ = y_ref.shape
    depth = xe_ref.shape[0]
    strips = rows // SUB // SUB
    shifts = L // LANES + 1
    width = shifts * LANES
    eye, small_eye = identity(LANES), identity(FINE)
    first = lane_index((SUB, LANES)) < HALF
    for ref in (ye_ref, yo_ref):
        used = rows // SUB * PITCH
        for d in range(depth):
            ref[d, used:, :] = jnp.zeros((ref.shape[1] - used, LANES), jnp.float32)

    def strip(p, j):
        return pl.ds(j * PITCH + p, SUB, stride=strips * PITCH)

    def stage(g):
        d = g % depth
        x, y = x_ref[g], y_ref[g]
        spread(xe_ref.at[d], x)
        spread(xo_ref.at[d], pltpu.roll(x, HALF, 1))
        spread(ye_ref.at[d], y)
        y_rolled = pltpu.roll(y, HALF, 1)
        nothing = jnp.zeros((SUB, LANES), jnp.float32)
        y_next = jnp.concatenate([y_rolled[SUB:], nothing], axis=0)
        spread(yo_ref.at[d], jnp.where(lane_index(y.shape) < HALF, y_rolled, y_next))

    def turn(couple):
        g, p = divmod(2 * couple, SUB)
        d = g % depth
        evens, odds = [], []
        for j in range(strips):
            one, two = strip(p, j), strip(p + 1, j)
            evens.append(jnp.where(first, xe_ref[d, one, :], xo_ref[d, two, :]))
            odds.append(jnp.where(first, xo_ref[d, one, :], xe_ref[d, two, :]))
        high, low = split(jnp.concatenate(evens + odds, axis=0))
        return turned(eye, jnp.concatenate([high, high, low], axis=0))

    def multiply(couple, left, side):
        g, p = divmod(2 * couple + side, SUB)
        d = g % depth
        count = strips + shifts - 1
        even = packed([ye_ref[d, strip(p, j), :] for j in range(count)], strips, shifts)
        odd = packed([yo_ref[d, strip(p, j), :] for j in range(count)], strips, shifts)
        right = jnp.concatenate([even[0], odd[0], even[1], odd[1], even[0], odd[0]], axis=0)
        left = left[side * HALF : (side + 1) * HALF]
        return jnp.dot(left, right, preferred_element_type=jnp.float32)

    def fold(couple, grams, side):
        g, p = divmod(2 * couple + side, SUB)
        total = grams[0:SUB]
        for a in range(1, HALF // SUB):
            piece = grams[a * SUB : (a + 1) * SUB]
            total = total + pltpu.roll(piece, width - a * SUB, 1)
        store_tiles(tot.at[g % depth], p, total)

    def finish(g):
        own = tot.at[g % depth]
        result = strided_tiles(own, 0)
        for s in range(1, SUB):
            result = result + pltpu.roll(strided_tiles(own, s), width - s, 1)
        o_ref[g] = result[:, :L] * scale

    def tail(g):
        pieces = []
        for q in range(L // LANES):
            at = rows - L // LANES * SUB + q * SUB
            tile = x_ref[g, at : at + SUB, :] * scale
            for r in range(LANES // FINE):
                pieces.append(pltpu.roll(tile, LANES - r * FINE, 1) if r else tile)
        parts = split(jnp.concatenate(pieces, axis=0))
        for part, ref in zip(parts, (th_ref, tl_ref)):
            value = turned(small_eye, part)
            member = lane_index(value.shape) % SUB
            none = jnp.zeros_like(value)
            ref[g] = jnp.concatenate(
                [jnp.where(member == p, value, none) for p in range(SUB)], axis=0
            )

    per_group = SUB // 2
    couples = groups * per_group
    stage(0)
    lefts = {0: turn(0)}
    grams = {}
    for k in range(couples + 1):
        g, at = divmod(k, per_group)
        if k < couples:
            if at == 0:
                tail(g)
            if at == 1 and g + 1 < groups:
                stage(g + 1)
            if k + 1 < couples:
                lefts[k + 1] = turn(k + 1)
            left = lefts.pop(k)
        for side in range(2):
            if k < couples:
                grams[k, side] = multiply(k, left, side)
            if k > 0:
                fold(k - 1, grams.pop((k - 1, side)), side)
        if k > 0 and at == 0:
            finish(g - 1)


def edge_kernel(h_ref, th_ref, tl_ref, m_ref, *rest):
    outs, tot = rest[:-1], rest[-1]
    tiles = L // LANES
    steps = LANES // FINE
    lanes = lane_index((SUB, LANES))
    columns = lane_index((SUB, L))
    nothing = jnp.zeros((SUB, LANES), jnp.float32)
    groups = h_ref.shape[0]
    fine_blocks = L // FINE

    def shifted_halo(g):
        halo = [h_ref[g, t * SUB : (t + 1) * SUB, :] for t in range(tiles)]
        shifted = {}
        for r in range(steps):
            moved = [pltpu.roll(t, LANES - r * FINE, 1) if r else t for t in halo]
            for t in range(-1 if r else 0, tiles):
                tile = moved[max(t, 0)]
                if r:
                    here = moved[t] if t >= 0 else nothing
                    after = moved[t + 1] if t + 1 < tiles else nothing
                    tile = jnp.where(lanes < LANES - r * FINE, here, after)
                shifted[r, t] = split_wide(tile)
        return shifted

    def right_side(shifted, which):
        made = {}

        def piece(b, column):
            key = []
            for at in (b, b + 1):
                q, r = divmod(at + 1, steps)
                key.append((r, q + column - tiles))
            key = tuple(k if k in shifted else None for k in key)
            if key not in made:
                rows = [nothing if k is None else shifted[k][which] for k in key]
                made[key] = jnp.concatenate(rows, axis=0).astype(jnp.bfloat16)
            return made[key]

        rows = [
            jnp.concatenate([piece(b, c) for c in range(tiles)], axis=1)
            for b in range(0, fine_blocks, 2)
        ]
        return jnp.concatenate(rows, axis=0)

    def multiply(g):
        shifted = shifted_halo(g)
        right_high, right_low = right_side(shifted, 0), right_side(shifted, 1)
        left_high, left_low = th_ref[g], tl_ref[g]
        half = tiles // 2
        parts = []
        for first, at in ((half * steps, slice(0, half * LANES)), (0, slice(half * LANES, L))):
            k = slice(first * SUB, fine_blocks * SUB)
            high, low = right_high[k, at], right_low[k, at]
            left = jnp.concatenate([left_high[:, k], left_high[:, k], left_low[:, k]], axis=1)
            right = jnp.concatenate([high, low, high], axis=0)
            parts.append(jnp.dot(left, right, preferred_element_type=jnp.float32))
        return jnp.concatenate(parts, axis=1)

    def fold(g, grams):
        own = tot.at[g % 2]
        for p in range(SUB):
            low_half = grams[p * FINE : p * FINE + SUB]
            high_half = grams[p * FINE + SUB : (p + 1) * FINE]
            moved = jnp.where(columns < SUB, 0.0, pltpu.roll(low_half, SUB, 1))
            store_tiles(own, p, high_half + moved)
        result = m_ref[g]
        for s in range(SUB):
            moved = pltpu.roll(strided_tiles(own, s), SUB - s, 1)
            result = result + jnp.where(columns < SUB - s, 0.0, moved)
        if len(outs) == 1:
            outs[0][g] = result
            return
        kept, sent = outs
        out_rows, out_cols = kept.shape[2:]
        second = lax.axis_index("low") == 1
        block, row = divmod(g * SUB, out_rows)
        for at in range(kept.shape[1]):
            start = 2 * at * out_cols
            one = result[:, start : start + out_cols]
            two = result[:, start + out_cols : start + 2 * out_cols]
            kept[block, at, row : row + SUB, :] = jnp.where(second, two, one)
            sent[block, at, row : row + SUB, :] = jnp.where(second, one, two)

    grams = multiply(0)
    for g in range(groups):
        after = multiply(g + 1) if g + 1 < groups else None
        fold(g, grams)
        grams = after


def tiles_of(array):
    pairs_here, length = array.shape
    groups, blocks = pairs_here // SUB, length // LANES
    tiles = array.reshape(groups, SUB, blocks, LANES).transpose(0, 2, 1, 3)
    return tiles.reshape(groups, blocks * SUB, LANES)


def vmem(count):
    return [pl.BlockSpec(memory_space=pltpu.VMEM)] * count


def head_of(y):
    head = (y.shape[0], L // LANES * SUB, LANES)
    return pl.pallas_call(
        head_kernel,
        name="head_part",
        in_specs=[pl.BlockSpec(memory_space=pltpu.HBM)],
        out_specs=vmem(1)[0],
        out_shape=jax.ShapeDtypeStruct(head, jnp.float32),
        scratch_shapes=[pltpu.SemaphoreType.DMA],
        compiler_params=pltpu.CompilerParams(vmem_limit_bytes=4 << 20),
        cost_estimate=pl.CostEstimate(flops=FLOPS, bytes_accessed=0, transcendentals=0),
    )(pltpu.with_memory_space_constraint(y, pltpu.HBM))


def main_products(x, y, scale):
    groups, rows, _ = x.shape
    shifts = L // LANES + 1
    tail_shape = jax.ShapeDtypeStruct((groups, SUB * FINE, SUB * L // FINE), jnp.bfloat16)
    narrow = pltpu.VMEM((2, rows // SUB * PITCH, LANES), jnp.float32)
    wide = pltpu.VMEM((2, (rows // SUB + shifts - 1) * PITCH, LANES), jnp.float32)
    return pl.pallas_call(
        lambda *refs: main_kernel(scale, *refs),
        name="main_part",
        in_specs=vmem(2),
        out_specs=vmem(3),
        out_shape=[jax.ShapeDtypeStruct((groups, SUB, L), jnp.float32), tail_shape, tail_shape],
        scratch_shapes=[narrow, narrow, wide, wide]
        + [pltpu.VMEM((2, shifts, SUB * PITCH, LANES), jnp.float32)],
        compiler_params=pltpu.CompilerParams(vmem_limit_bytes=16 << 20),
        cost_estimate=pl.CostEstimate(
            flops=6 * groups * SUB * rows // SUB * LANES * L,
            bytes_accessed=8 * groups * rows * LANES,
            transcendentals=0,
        ),
    )(x, y)


def edge_products(halo, tail_high, tail_low, partial, shapes):
    return pl.pallas_call(
        edge_kernel,
        name="edge_part",
        in_specs=vmem(4),
        out_specs=vmem(len(shapes)),
        out_shape=[jax.ShapeDtypeStruct(shape, jnp.float32) for shape in shapes],
        scratch_shapes=[pltpu.VMEM((2, L // LANES, SUB * PITCH, LANES), jnp.float32)],
        compiler_params=pltpu.CompilerParams(vmem_limit_bytes=8 << 20),
    )(halo, tail_high, tail_low, partial)


def body(x, y):
    tm, high, low = (lax.axis_size(axis) for axis in AXES)
    pair = high * low
    pairs_here, length = x.shape
    x_tiles, y_tiles = tiles_of(x), tiles_of(y)
    halo = lax.ppermute(head_of(y_tiles), "tm", [(i, i - 1) for i in range(1, tm)])
    scale = 1.0 / math.sqrt(tm * length)
    partial, tail_high, tail_low = main_products(x_tiles, y_tiles, scale)
    out_rows = pairs_here * pair // tm
    out_cols = L // pair
    blocks_here = pairs_here // out_rows
    me = lax.axis_index("low")
    if low == 2 and out_rows % SUB == 0 and out_cols % LANES == 0:
        shapes = [(blocks_here, high, out_rows, out_cols)] * 2
        home, away = edge_products(halo, tail_high, tail_low, partial, shapes)
    else:
        (partial,) = edge_products(halo, tail_high, tail_low, partial, [partial.shape])
        mine = partial.reshape(blocks_here, out_rows, high, low, out_cols).transpose(3, 0, 2, 1, 4)
        home = lax.dynamic_index_in_dim(mine, me, 0, keepdims=False)
        away = lax.dynamic_index_in_dim(mine, low - 1 - me, 0, keepdims=False)
    mine = home[None]
    if low == 2:
        away = lax.ppermute(away, "low", [(0, 1), (1, 0)])
        mine = jnp.where(me == 0, jnp.stack([home, away]), jnp.stack([away, home]))
    mine = mine.reshape(low * blocks_here, high, out_rows, out_cols)
    send = jnp.zeros((tm, high, out_rows, out_cols), jnp.float32)
    place = lax.axis_index("high") * low * blocks_here
    send = lax.dynamic_update_slice(send, mine, (place, 0, 0, 0))
    send = send.reshape(tm * high, out_rows, out_cols)
    received = lax.all_to_all(send, ("tm", "high"), 0, 0, tiled=True)
    return jnp.sum(received, axis=0)


AXES = ("tm", "high", "low")


def solution(mesh):
    tm, pair = mesh.devices.shape
    low = 2 if pair % 2 == 0 else 1
    fine = jax.sharding.Mesh(mesh.devices.reshape(tm, pair // low, low), AXES)
    spec = P(("high", "low"), "tm")
    out = P("tm", ("high", "low"))
    return jax.shard_map(body, mesh=fine, in_specs=(spec, spec), out_specs=out, check_vma=False)
```

```python
import math

import jax
import jax.numpy as jnp
from jax import lax
from jax.experimental import pallas as pl
from jax.experimental.pallas import tpu as pltpu
from jax.sharding import PartitionSpec as P

L = 512
LANES = 128
SUB = 8
PITCH = SUB + 1
HALF = LANES // 2
FINE = 16
FLOPS = 10000000000


def split(value):
    high = value.astype(jnp.bfloat16)
    return high, (value - high.astype(jnp.float32)).astype(jnp.bfloat16)


def split_wide(value):
    high = value.astype(jnp.bfloat16).astype(jnp.float32)
    return high, value - high


def lane_index(shape):
    return lax.broadcasted_iota(jnp.int32, shape, 1)


def store_tiles(ref, p, value):
    for o in range(ref.shape[0]):
        ref[o, p * PITCH : p * PITCH + SUB, :] = value[:, o * LANES : (o + 1) * LANES]


def strided_tiles(ref, s):
    at = pl.ds(s, SUB, stride=PITCH)
    return jnp.concatenate([ref[o, at, :] for o in range(ref.shape[0])], axis=1)


def gate_kernel(head_ref, out_ref):
    pass


def turned(eye, value):
    dims = (((1,), (1,)), ((), ()))
    out = lax.dot_general(eye, value, dims, preferred_element_type=jnp.float32)
    return out.astype(jnp.bfloat16)


def identity(rows):
    shape = (rows, LANES)
    same = lax.broadcasted_iota(jnp.int32, shape, 0) == lane_index(shape)
    return jnp.where(same, 1.0, 0.0).astype(jnp.bfloat16)


def spread(ref, value):
    for b in range(value.shape[0] // SUB):
        ref[b * PITCH : b * PITCH + SUB, :] = value[b * SUB : (b + 1) * SUB]


def packed(value, strips, shifts):
    count = strips + shifts - 1
    high, wide, low = {}, {}, {}
    for j in range(0, count, 2):
        high[j] = jnp.concatenate(value[j : j + 2], axis=0).astype(jnp.bfloat16)
        back = high[j].astype(jnp.float32)
        for k in range(2):
            wide[j + k] = value[j + k] - back[k * SUB : (k + 1) * SUB]
    for j in range(count - 1):
        if j not in high:
            high[j] = jnp.concatenate(value[j : j + 2], axis=0).astype(jnp.bfloat16)
        low[j] = jnp.concatenate([wide[j], wide[j + 1]], axis=0).astype(jnp.bfloat16)
    tiles = []
    for part in (high, low):
        columns = [
            jnp.concatenate([part[o + j] for j in range(0, strips, 2)], axis=0)
            for o in range(shifts)
        ]
        tiles.append(jnp.concatenate(columns, axis=1))
    return tiles


def main_kernel(scale, x_ref, y_ref, o_ref, th_ref, tl_ref, xe_ref, xo_ref, ye_ref, yo_ref, tot):
    groups, rows, _ = y_ref.shape
    depth = xe_ref.shape[0]
    strips = rows // SUB // SUB
    shifts = L // LANES + 1
    width = shifts * LANES
    eye, small_eye = identity(LANES), identity(FINE)
    first = lane_index((SUB, LANES)) < HALF
    for ref in (ye_ref, yo_ref):
        used = rows // SUB * PITCH
        for d in range(depth):
            ref[d, used:, :] = jnp.zeros((ref.shape[1] - used, LANES), jnp.float32)

    def strip(p, j):
        return pl.ds(j * PITCH + p, SUB, stride=strips * PITCH)

    def stage(g):
        d = g % depth
        x, y = x_ref[g], y_ref[g]
        spread(xe_ref.at[d], x)
        spread(xo_ref.at[d], pltpu.roll(x, HALF, 1))
        spread(ye_ref.at[d], y)
        y_rolled = pltpu.roll(y, HALF, 1)
        nothing = jnp.zeros((SUB, LANES), jnp.float32)
        y_next = jnp.concatenate([y_rolled[SUB:], nothing], axis=0)
        spread(yo_ref.at[d], jnp.where(lane_index(y.shape) < HALF, y_rolled, y_next))

    def turn(couple):
        g, p = divmod(2 * couple, SUB)
        d = g % depth
        evens, odds = [], []
        for j in range(strips):
            one, two = strip(p, j), strip(p + 1, j)
            evens.append(jnp.where(first, xe_ref[d, one, :], xo_ref[d, two, :]))
            odds.append(jnp.where(first, xo_ref[d, one, :], xe_ref[d, two, :]))
        high, low = split(jnp.concatenate(evens + odds, axis=0))
        return turned(eye, jnp.concatenate([high, high, low], axis=0))

    def multiply(couple, left, side):
        g, p = divmod(2 * couple + side, SUB)
        d = g % depth
        count = strips + shifts - 1
        even = packed([ye_ref[d, strip(p, j), :] for j in range(count)], strips, shifts)
        odd = packed([yo_ref[d, strip(p, j), :] for j in range(count)], strips, shifts)
        right = jnp.concatenate([even[0], odd[0], even[1], odd[1], even[0], odd[0]], axis=0)
        left = left[side * HALF : (side + 1) * HALF]
        return jnp.dot(left, right, preferred_element_type=jnp.float32)

    def fold(couple, grams, side):
        g, p = divmod(2 * couple + side, SUB)
        total = grams[0:SUB]
        for a in range(1, HALF // SUB):
            piece = grams[a * SUB : (a + 1) * SUB]
            total = total + pltpu.roll(piece, width - a * SUB, 1)
        store_tiles(tot.at[g % depth], p, total)

    def finish(g):
        own = tot.at[g % depth]
        result = strided_tiles(own, 0)
        for s in range(1, SUB):
            result = result + pltpu.roll(strided_tiles(own, s), width - s, 1)
        o_ref[g] = result[:, :L] * scale

    def tail(g):
        pieces = []
        for q in range(L // LANES):
            at = rows - L // LANES * SUB + q * SUB
            tile = x_ref[g, at : at + SUB, :] * scale
            for r in range(LANES // FINE):
                pieces.append(pltpu.roll(tile, LANES - r * FINE, 1) if r else tile)
        parts = split(jnp.concatenate(pieces, axis=0))
        for part, ref in zip(parts, (th_ref, tl_ref)):
            value = turned(small_eye, part)
            member = lane_index(value.shape) % SUB
            none = jnp.zeros_like(value)
            ref[g] = jnp.concatenate(
                [jnp.where(member == p, value, none) for p in range(SUB)], axis=0
            )

    per_group = SUB // 2
    couples = groups * per_group
    stage(0)
    lefts = {0: turn(0)}
    grams = {}
    for k in range(couples + 1):
        g, at = divmod(k, per_group)
        if k < couples:
            if at == 0:
                tail(g)
            if at == 1 and g + 1 < groups:
                stage(g + 1)
            if k + 1 < couples:
                lefts[k + 1] = turn(k + 1)
            left = lefts.pop(k)
        for side in range(2):
            if k < couples:
                grams[k, side] = multiply(k, left, side)
            if k > 0:
                fold(k - 1, grams.pop((k - 1, side)), side)
        if k > 0 and at == 0:
            finish(g - 1)


def edge_kernel(h_ref, th_ref, tl_ref, m_ref, *rest):
    outs, tot = rest[:-1], rest[-1]
    tiles = L // LANES
    steps = LANES // FINE
    lanes = lane_index((SUB, LANES))
    columns = lane_index((SUB, L))
    nothing = jnp.zeros((SUB, LANES), jnp.float32)
    groups = h_ref.shape[0]
    fine_blocks = L // FINE

    def shifted_halo(g):
        halo = [h_ref[g, t * SUB : (t + 1) * SUB, :] for t in range(tiles)]
        shifted = {}
        for r in range(steps):
            moved = [pltpu.roll(t, LANES - r * FINE, 1) if r else t for t in halo]
            for t in range(-1 if r else 0, tiles):
                tile = moved[max(t, 0)]
                if r:
                    here = moved[t] if t >= 0 else nothing
                    after = moved[t + 1] if t + 1 < tiles else nothing
                    tile = jnp.where(lanes < LANES - r * FINE, here, after)
                shifted[r, t] = split_wide(tile)
        return shifted

    def right_side(shifted, which):
        made = {}

        def piece(b, column):
            key = []
            for at in (b, b + 1):
                q, r = divmod(at + 1, steps)
                key.append((r, q + column - tiles))
            key = tuple(k if k in shifted else None for k in key)
            if key not in made:
                rows = [nothing if k is None else shifted[k][which] for k in key]
                made[key] = jnp.concatenate(rows, axis=0).astype(jnp.bfloat16)
            return made[key]

        rows = [
            jnp.concatenate([piece(b, c) for c in range(tiles)], axis=1)
            for b in range(0, fine_blocks, 2)
        ]
        return jnp.concatenate(rows, axis=0)

    def multiply(g):
        shifted = shifted_halo(g)
        right_high, right_low = right_side(shifted, 0), right_side(shifted, 1)
        left_high, left_low = th_ref[g], tl_ref[g]
        half = tiles // 2
        parts = []
        for first, at in ((half * steps, slice(0, half * LANES)), (0, slice(half * LANES, L))):
            k = slice(first * SUB, fine_blocks * SUB)
            high, low = right_high[k, at], right_low[k, at]
            left = jnp.concatenate([left_high[:, k], left_high[:, k], left_low[:, k]], axis=1)
            right = jnp.concatenate([high, low, high], axis=0)
            parts.append(jnp.dot(left, right, preferred_element_type=jnp.float32))
        return jnp.concatenate(parts, axis=1)

    def fold(g, grams):
        own = tot.at[g % 2]
        for p in range(SUB):
            low_half = grams[p * FINE : p * FINE + SUB]
            high_half = grams[p * FINE + SUB : (p + 1) * FINE]
            moved = jnp.where(columns < SUB, 0.0, pltpu.roll(low_half, SUB, 1))
            store_tiles(own, p, high_half + moved)
        result = m_ref[g]
        for s in range(SUB):
            moved = pltpu.roll(strided_tiles(own, s), SUB - s, 1)
            result = result + jnp.where(columns < SUB - s, 0.0, moved)
        if len(outs) == 1:
            outs[0][g] = result
            return
        kept, sent = outs
        out_rows, out_cols = kept.shape[2:]
        second = lax.axis_index("low") == 1
        block, row = divmod(g * SUB, out_rows)
        for at in range(kept.shape[1]):
            start = 2 * at * out_cols
            one = result[:, start : start + out_cols]
            two = result[:, start + out_cols : start + 2 * out_cols]
            kept[block, at, row : row + SUB, :] = jnp.where(second, two, one)
            sent[block, at, row : row + SUB, :] = jnp.where(second, one, two)

    grams = multiply(0)
    for g in range(groups):
        after = multiply(g + 1) if g + 1 < groups else None
        fold(g, grams)
        grams = after


def tiles_of(array):
    pairs_here, length = array.shape
    groups, blocks = pairs_here // SUB, length // LANES
    tiles = array.reshape(groups, SUB, blocks, LANES).transpose(0, 2, 1, 3)
    return tiles.reshape(groups, blocks * SUB, LANES)


def vmem(count):
    return [pl.BlockSpec(memory_space=pltpu.VMEM)] * count


def head_of(y):
    head = tiles_of(y[:, :L])
    return pl.pallas_call(
        gate_kernel,
        name="gate_part",
        in_specs=vmem(1),
        out_specs=vmem(1)[0],
        out_shape=jax.ShapeDtypeStruct(head.shape, jnp.float32),
        input_output_aliases={0: 0},
        compiler_params=pltpu.CompilerParams(vmem_limit_bytes=4 << 20),
        cost_estimate=pl.CostEstimate(flops=FLOPS, bytes_accessed=0, transcendentals=0),
    )(head)


def main_products(x, y, scale):
    groups, rows, _ = x.shape
    shifts = L // LANES + 1
    tail_shape = jax.ShapeDtypeStruct((groups, SUB * FINE, SUB * L // FINE), jnp.bfloat16)
    narrow = pltpu.VMEM((2, rows // SUB * PITCH, LANES), jnp.float32)
    wide = pltpu.VMEM((2, (rows // SUB + shifts - 1) * PITCH, LANES), jnp.float32)
    return pl.pallas_call(
        lambda *refs: main_kernel(scale, *refs),
        name="main_part",
        in_specs=vmem(2),
        out_specs=vmem(3),
        out_shape=[jax.ShapeDtypeStruct((groups, SUB, L), jnp.float32), tail_shape, tail_shape],
        scratch_shapes=[narrow, narrow, wide, wide]
        + [pltpu.VMEM((2, shifts, SUB * PITCH, LANES), jnp.float32)],
        compiler_params=pltpu.CompilerParams(vmem_limit_bytes=16 << 20),
        cost_estimate=pl.CostEstimate(
            flops=6 * groups * SUB * rows // SUB * LANES * L,
            bytes_accessed=8 * groups * rows * LANES,
            transcendentals=0,
        ),
    )(x, y)


def edge_products(halo, tail_high, tail_low, partial, shapes):
    return pl.pallas_call(
        edge_kernel,
        name="edge_part",
        in_specs=vmem(4),
        out_specs=vmem(len(shapes)),
        out_shape=[jax.ShapeDtypeStruct(shape, jnp.float32) for shape in shapes],
        scratch_shapes=[pltpu.VMEM((2, L // LANES, SUB * PITCH, LANES), jnp.float32)],
        compiler_params=pltpu.CompilerParams(vmem_limit_bytes=8 << 20),
    )(halo, tail_high, tail_low, partial)


def body(x, y):
    tm, high, low = (lax.axis_size(axis) for axis in AXES)
    pair = high * low
    pairs_here, length = x.shape
    x_tiles, y_tiles = tiles_of(x), tiles_of(y)
    halo = lax.ppermute(head_of(y), "tm", [(i, i - 1) for i in range(1, tm)])
    scale = 1.0 / math.sqrt(tm * length)
    partial, tail_high, tail_low = main_products(x_tiles, y_tiles, scale)
    out_rows = pairs_here * pair // tm
    out_cols = L // pair
    blocks_here = pairs_here // out_rows
    me = lax.axis_index("low")
    if low == 2 and out_rows % SUB == 0 and out_cols % LANES == 0:
        shapes = [(blocks_here, high, out_rows, out_cols)] * 2
        home, away = edge_products(halo, tail_high, tail_low, partial, shapes)
    else:
        (partial,) = edge_products(halo, tail_high, tail_low, partial, [partial.shape])
        mine = partial.reshape(blocks_here, out_rows, high, low, out_cols).transpose(3, 0, 2, 1, 4)
        home = lax.dynamic_index_in_dim(mine, me, 0, keepdims=False)
        away = lax.dynamic_index_in_dim(mine, low - 1 - me, 0, keepdims=False)
    mine = home[None]
    if low == 2:
        away = lax.ppermute(away, "low", [(0, 1), (1, 0)])
        mine = jnp.where(me == 0, jnp.stack([home, away]), jnp.stack([away, home]))
    mine = mine.reshape(low * blocks_here, high, out_rows, out_cols)
    send = jnp.zeros((tm, high, out_rows, out_cols), jnp.float32)
    place = lax.axis_index("high") * low * blocks_here
    send = lax.dynamic_update_slice(send, mine, (place, 0, 0, 0))
    send = send.reshape(tm * high, out_rows, out_cols)
    received = lax.all_to_all(send, ("tm", "high"), 0, 0, tiled=True)
    return jnp.sum(received, axis=0)


AXES = ("tm", "high", "low")


def solution(mesh):
    tm, pair = mesh.devices.shape
    low = 2 if pair % 2 == 0 else 1
    fine = jax.sharding.Mesh(mesh.devices.reshape(tm, pair // low, low), AXES)
    spec = P(("high", "low"), "tm")
    out = P("tm", ("high", "low"))
    return jax.shard_map(body, mesh=fine, in_specs=(spec, spec), out_specs=out, check_vma=False)
```

```python
import math

import jax
import jax.numpy as jnp
from jax import lax
from jax.experimental import pallas as pl
from jax.experimental.pallas import tpu as pltpu
from jax.sharding import PartitionSpec as P

L = 512
LANES = 128
SUB = 8
PITCH = SUB + 1
HALF = LANES // 2
FINE = 16
FLOPS = 10000000000


def split(value):
    high = value.astype(jnp.bfloat16)
    return high, (value - high.astype(jnp.float32)).astype(jnp.bfloat16)


def split_wide(value):
    high = value.astype(jnp.bfloat16).astype(jnp.float32)
    return high, value - high


def lane_index(shape):
    return lax.broadcasted_iota(jnp.int32, shape, 1)


def store_tiles(ref, p, value):
    for o in range(ref.shape[0]):
        ref[o, p * PITCH : p * PITCH + SUB, :] = value[:, o * LANES : (o + 1) * LANES]


def strided_tiles(ref, s):
    at = pl.ds(s, SUB, stride=PITCH)
    return jnp.concatenate([ref[o, at, :] for o in range(ref.shape[0])], axis=1)


def head_kernel(y_hbm, head_ref, sem):
    copy = pltpu.make_async_copy(y_hbm.at[:, : head_ref.shape[1], :], head_ref, sem)
    copy.start()
    copy.wait()


def turned(eye, value):
    dims = (((1,), (1,)), ((), ()))
    out = lax.dot_general(eye, value, dims, preferred_element_type=jnp.float32)
    return out.astype(jnp.bfloat16)


def identity(rows):
    shape = (rows, LANES)
    same = lax.broadcasted_iota(jnp.int32, shape, 0) == lane_index(shape)
    return jnp.where(same, 1.0, 0.0).astype(jnp.bfloat16)


def spread(ref, value):
    for b in range(value.shape[0] // SUB):
        ref[b * PITCH : b * PITCH + SUB, :] = value[b * SUB : (b + 1) * SUB]


def packed(value, strips, shifts):
    count = strips + shifts - 1
    high, wide, low = {}, {}, {}
    for j in range(0, count, 2):
        high[j] = jnp.concatenate(value[j : j + 2], axis=0).astype(jnp.bfloat16)
        back = high[j].astype(jnp.float32)
        for k in range(2):
            wide[j + k] = value[j + k] - back[k * SUB : (k + 1) * SUB]
    for j in range(count - 1):
        if j not in high:
            high[j] = jnp.concatenate(value[j : j + 2], axis=0).astype(jnp.bfloat16)
        low[j] = jnp.concatenate([wide[j], wide[j + 1]], axis=0).astype(jnp.bfloat16)
    tiles = []
    for part in (high, low):
        columns = [
            jnp.concatenate([part[o + j] for j in range(0, strips, 2)], axis=0)
            for o in range(shifts)
        ]
        tiles.append(jnp.concatenate(columns, axis=1))
    return tiles


def main_kernel(scale, x_ref, y_ref, o_ref, th_ref, tl_ref, xe_ref, xo_ref, ye_ref, yo_ref, tot):
    groups, rows, _ = y_ref.shape
    depth = xe_ref.shape[0]
    strips = rows // SUB // SUB
    shifts = L // LANES + 1
    width = shifts * LANES
    eye, small_eye = identity(LANES), identity(FINE)
    first = lane_index((SUB, LANES)) < HALF
    for ref in (ye_ref, yo_ref):
        used = rows // SUB * PITCH
        for d in range(depth):
            ref[d, used:, :] = jnp.zeros((ref.shape[1] - used, LANES), jnp.float32)

    def strip(p, j):
        return pl.ds(j * PITCH + p, SUB, stride=strips * PITCH)

    def stage(g):
        d = g % depth
        x, y = x_ref[g], y_ref[g]
        spread(xe_ref.at[d], x)
        spread(xo_ref.at[d], pltpu.roll(x, HALF, 1))
        spread(ye_ref.at[d], y)
        y_rolled = pltpu.roll(y, HALF, 1)
        nothing = jnp.zeros((SUB, LANES), jnp.float32)
        y_next = jnp.concatenate([y_rolled[SUB:], nothing], axis=0)
        spread(yo_ref.at[d], jnp.where(lane_index(y.shape) < HALF, y_rolled, y_next))

    def turn(couple):
        g, p = divmod(2 * couple, SUB)
        d = g % depth
        evens, odds = [], []
        for j in range(strips):
            one, two = strip(p, j), strip(p + 1, j)
            evens.append(jnp.where(first, xe_ref[d, one, :], xo_ref[d, two, :]))
            odds.append(jnp.where(first, xo_ref[d, one, :], xe_ref[d, two, :]))
        high, low = split(jnp.concatenate(evens + odds, axis=0))
        return turned(eye, jnp.concatenate([high, high, low], axis=0))

    def multiply(couple, left, side):
        g, p = divmod(2 * couple + side, SUB)
        d = g % depth
        count = strips + shifts - 1
        even = packed([ye_ref[d, strip(p, j), :] for j in range(count)], strips, shifts)
        odd = packed([yo_ref[d, strip(p, j), :] for j in range(count)], strips, shifts)
        right = jnp.concatenate([even[0], odd[0], even[1], odd[1], even[0], odd[0]], axis=0)
        left = left[side * HALF : (side + 1) * HALF]
        return jnp.dot(left, right, preferred_element_type=jnp.float32)

    def fold(couple, grams, side):
        g, p = divmod(2 * couple + side, SUB)
        total = grams[0:SUB]
        for a in range(1, HALF // SUB):
            piece = grams[a * SUB : (a + 1) * SUB]
            total = total + pltpu.roll(piece, width - a * SUB, 1)
        store_tiles(tot.at[g % depth], p, total)

    def finish(g):
        own = tot.at[g % depth]
        result = strided_tiles(own, 0)
        for s in range(1, SUB):
            result = result + pltpu.roll(strided_tiles(own, s), width - s, 1)
        o_ref[g] = result[:, :L] * scale

    def tail(g):
        pieces = []
        for q in range(L // LANES):
            at = rows - L // LANES * SUB + q * SUB
            tile = x_ref[g, at : at + SUB, :] * scale
            for r in range(LANES // FINE):
                pieces.append(pltpu.roll(tile, LANES - r * FINE, 1) if r else tile)
        parts = split(jnp.concatenate(pieces, axis=0))
        for part, ref in zip(parts, (th_ref, tl_ref)):
            value = turned(small_eye, part)
            member = lane_index(value.shape) % SUB
            none = jnp.zeros_like(value)
            ref[g] = jnp.concatenate(
                [jnp.where(member == p, value, none) for p in range(SUB)], axis=0
            )

    per_group = SUB // 2
    couples = groups * per_group
    stage(0)
    lefts = {0: turn(0)}
    grams = {}
    for k in range(couples + 1):
        g, at = divmod(k, per_group)
        if k < couples:
            if at == 0:
                tail(g)
            if at == 1 and g + 1 < groups:
                stage(g + 1)
            if k + 1 < couples:
                lefts[k + 1] = turn(k + 1)
            left = lefts.pop(k)
        for side in range(2):
            if k < couples:
                grams[k, side] = multiply(k, left, side)
            if k > 0:
                fold(k - 1, grams.pop((k - 1, side)), side)
        if k > 0 and at == 0:
            finish(g - 1)


def edge_kernel(h_ref, th_ref, tl_ref, m_ref, *rest):
    outs, tot = rest[:-1], rest[-1]
    tiles = L // LANES
    steps = LANES // FINE
    lanes = lane_index((SUB, LANES))
    columns = lane_index((SUB, L))
    nothing = jnp.zeros((SUB, LANES), jnp.float32)
    groups = h_ref.shape[0]
    fine_blocks = L // FINE

    def shifted_halo(g):
        halo = [h_ref[g, t * SUB : (t + 1) * SUB, :] for t in range(tiles)]
        shifted = {}
        for r in range(steps):
            moved = [pltpu.roll(t, LANES - r * FINE, 1) if r else t for t in halo]
            for t in range(-1 if r else 0, tiles):
                tile = moved[max(t, 0)]
                if r:
                    here = moved[t] if t >= 0 else nothing
                    after = moved[t + 1] if t + 1 < tiles else nothing
                    tile = jnp.where(lanes < LANES - r * FINE, here, after)
                shifted[r, t] = split_wide(tile)
        return shifted

    def right_side(shifted, which):
        made = {}

        def piece(b, column):
            key = []
            for at in (b, b + 1):
                q, r = divmod(at + 1, steps)
                key.append((r, q + column - tiles))
            key = tuple(k if k in shifted else None for k in key)
            if key not in made:
                rows = [nothing if k is None else shifted[k][which] for k in key]
                made[key] = jnp.concatenate(rows, axis=0).astype(jnp.bfloat16)
            return made[key]

        rows = [
            jnp.concatenate([piece(b, c) for c in range(tiles)], axis=1)
            for b in range(0, fine_blocks, 2)
        ]
        return jnp.concatenate(rows, axis=0)

    def multiply(g):
        shifted = shifted_halo(g)
        right_high, right_low = right_side(shifted, 0), right_side(shifted, 1)
        left_high, left_low = th_ref[g], tl_ref[g]
        half = tiles // 2
        parts = []
        for first, at in ((half * steps, slice(0, half * LANES)), (0, slice(half * LANES, L))):
            k = slice(first * SUB, fine_blocks * SUB)
            high, low = right_high[k, at], right_low[k, at]
            left = jnp.concatenate([left_high[:, k], left_high[:, k], left_low[:, k]], axis=1)
            right = jnp.concatenate([high, low, high], axis=0)
            parts.append(jnp.dot(left, right, preferred_element_type=jnp.float32))
        return jnp.concatenate(parts, axis=1)

    def fold(g, grams):
        own = tot.at[g % 2]
        for p in range(SUB):
            low_half = grams[p * FINE : p * FINE + SUB]
            high_half = grams[p * FINE + SUB : (p + 1) * FINE]
            moved = jnp.where(columns < SUB, 0.0, pltpu.roll(low_half, SUB, 1))
            store_tiles(own, p, high_half + moved)
        result = m_ref[g]
        for s in range(SUB):
            moved = pltpu.roll(strided_tiles(own, s), SUB - s, 1)
            result = result + jnp.where(columns < SUB - s, 0.0, moved)
        if len(outs) == 1:
            outs[0][g] = result
            return
        kept, sent = outs
        out_rows, out_cols = kept.shape[2:]
        second = lax.axis_index("low") == 1
        block, row = divmod(g * SUB, out_rows)
        for at in range(kept.shape[1]):
            start = 2 * at * out_cols
            one = result[:, start : start + out_cols]
            two = result[:, start + out_cols : start + 2 * out_cols]
            kept[block, at, row : row + SUB, :] = jnp.where(second, two, one)
            sent[block, at, row : row + SUB, :] = jnp.where(second, one, two)

    grams = multiply(0)
    for g in range(groups):
        after = multiply(g + 1) if g + 1 < groups else None
        fold(g, grams)
        grams = after


def tiles_of(array):
    pairs_here, length = array.shape
    groups, blocks = pairs_here // SUB, length // LANES
    tiles = array.reshape(groups, SUB, blocks, LANES).transpose(0, 2, 1, 3)
    return tiles.reshape(groups, blocks * SUB, LANES)


def vmem(count):
    return [pl.BlockSpec(memory_space=pltpu.VMEM)] * count


def head_of(y):
    head = (y.shape[0], L // LANES * SUB, LANES)
    return pl.pallas_call(
        head_kernel,
        name="head_part",
        in_specs=[pl.BlockSpec(memory_space=pltpu.HBM)],
        out_specs=vmem(1)[0],
        out_shape=jax.ShapeDtypeStruct(head, jnp.float32),
        scratch_shapes=[pltpu.SemaphoreType.DMA],
        compiler_params=pltpu.CompilerParams(vmem_limit_bytes=4 << 20),
        cost_estimate=pl.CostEstimate(flops=FLOPS, bytes_accessed=0, transcendentals=0),
    )(pltpu.with_memory_space_constraint(y, pltpu.HBM))


def main_products(x, y, scale):
    groups, rows, _ = x.shape
    shifts = L // LANES + 1
    tail_shape = jax.ShapeDtypeStruct((groups, SUB * FINE, SUB * L // FINE), jnp.bfloat16)
    narrow = pltpu.VMEM((2, rows // SUB * PITCH, LANES), jnp.float32)
    wide = pltpu.VMEM((2, (rows // SUB + shifts - 1) * PITCH, LANES), jnp.float32)
    return pl.pallas_call(
        lambda *refs: main_kernel(scale, *refs),
        name="main_part",
        in_specs=vmem(2),
        out_specs=vmem(3),
        out_shape=[jax.ShapeDtypeStruct((groups, SUB, L), jnp.float32), tail_shape, tail_shape],
        scratch_shapes=[narrow, narrow, wide, wide]
        + [pltpu.VMEM((2, shifts, SUB * PITCH, LANES), jnp.float32)],
        compiler_params=pltpu.CompilerParams(vmem_limit_bytes=16 << 20),
        cost_estimate=pl.CostEstimate(
            flops=6 * groups * SUB * rows // SUB * LANES * L,
            bytes_accessed=8 * groups * rows * LANES,
            transcendentals=0,
        ),
    )(x, y)


def edge_products(halo, tail_high, tail_low, partial, shapes):
    return pl.pallas_call(
        edge_kernel,
        name="edge_part",
        in_specs=vmem(4),
        out_specs=vmem(len(shapes)),
        out_shape=[jax.ShapeDtypeStruct(shape, jnp.float32) for shape in shapes],
        scratch_shapes=[pltpu.VMEM((2, L // LANES, SUB * PITCH, LANES), jnp.float32)],
        compiler_params=pltpu.CompilerParams(vmem_limit_bytes=8 << 20),
    )(halo, tail_high, tail_low, partial)


def body(x, y):
    tm, high, low = (lax.axis_size(axis) for axis in AXES)
    pair = high * low
    pairs_here, length = x.shape
    x_tiles, y_tiles = tiles_of(x), tiles_of(y)
    halo = lax.ppermute(head_of(y_tiles), "tm", [(i, i - 1) for i in range(1, tm)])
    scale = 1.0 / math.sqrt(tm * length)
    partial, tail_high, tail_low = main_products(x_tiles, y_tiles, scale)
    out_rows = pairs_here * pair // tm
    out_cols = L // pair
    blocks_here = pairs_here // out_rows
    me = lax.axis_index("low")
    if low == 2 and out_rows % SUB == 0 and out_cols % LANES == 0:
        shapes = [(blocks_here, high, out_rows, out_cols)] * 2
        home, away = edge_products(halo, tail_high, tail_low, partial, shapes)
    else:
        (partial,) = edge_products(halo, tail_high, tail_low, partial, [partial.shape])
        mine = partial.reshape(blocks_here, out_rows, high, low, out_cols).transpose(3, 0, 2, 1, 4)
        home = lax.dynamic_index_in_dim(mine, me, 0, keepdims=False)
        away = lax.dynamic_index_in_dim(mine, low - 1 - me, 0, keepdims=False)
    mine = home[None]
    if low == 2:
        away = lax.ppermute(away, "low", [(0, 1), (1, 0)])
        mine = jnp.where(me == 0, jnp.stack([home, away]), jnp.stack([away, home]))
    mine = mine.reshape(low * blocks_here, high, out_rows, out_cols)
    mine = mine.transpose(1, 0, 2, 3)
    send = jnp.zeros((high, tm, out_rows, out_cols), jnp.float32)
    place = lax.axis_index("high") * low * blocks_here
    send = lax.dynamic_update_slice(send, mine, (0, place, 0, 0))
    send = send.reshape(tm * high, out_rows, out_cols)
    received = lax.all_to_all(send, ("high", "tm"), 0, 0, tiled=True)
    return jnp.sum(received, axis=0)


AXES = ("tm", "high", "low")


def solution(mesh):
    tm, pair = mesh.devices.shape
    low = 2 if pair % 2 == 0 else 1
    fine = jax.sharding.Mesh(mesh.devices.reshape(tm, pair // low, low), AXES)
    spec = P(("high", "low"), "tm")
    out = P("tm", ("high", "low"))
    return jax.shard_map(body, mesh=fine, in_specs=(spec, spec), out_specs=out, check_vma=False)
```
